512 devices in a mesh: section: 32 (over z, core), seq: 16 (over x, y).
Axes of the slice: x: 4, y: 4, z: 16, core: 2. Of those that a mesh axis runs over, the one named last changes fastest.
Arguments:
- layer_input: bfloat16 [32, 3, 4096, 768], P('section', None, 'seq'), may hold values from -6 to 6
- grad_out: bfloat16 [32, 3, 4096, 768], P('section', None, 'seq'), may hold values from -6 to 6
- gate_weight: bfloat16 [768, 768], P('seq'), may hold values from -0.21875 to 0.21875
- mix_in_right: bfloat16 [64, 64, 64], P('seq'), may hold values from -0.75 to 0.75
- mix_in_left: bfloat16 [64, 64, 64], P('seq'), may hold values from -0.75 to 0.75
- mix_out_left: bfloat16 [64, 64, 64], P('seq'), may hold values from -0.75 to 0.75
- mix_out_right: bfloat16 [64, 64, 64], P('seq'), may hold values from -0.75 to 0.75
- kernel: bfloat16 [4096, 768], P('seq'), may hold values from -5 to 5
Outputs:
- input_grad: bfloat16 [32, 3, 4096, 768], P('section', None, 'seq')
- weight_grad: float32 [768, 768], P('seq')
- kernel_grad: bfloat16 [4096, 768], P('seq')
The draws below stay inside these ranges and needn't reach their ends.
All inputs are finite; a program needn't handle non-finite values.
Results may differ from the reference program's by a relative error of at most 0.007.
Values may be sent and summed in bfloat16 or wider, within the bound.
A program may use at most 64 MiB of HBM per device.

```python
import math
import jax
import jax.numpy as jnp
from jax import lax

D = 768
BLOCK = 64
BATCH = 3
SEQ = 4096
REPLICAS = 32


def raised(drawn, key, source, target, shards_of, factor):
    def block_of(position):
        return (jnp.arange(drawn.shape[position]) // (drawn.shape[position] // shards_of)).reshape((-1,) + (1,) * (drawn.ndim - 1 - position))

    one_side = jax.random.permutation(key, shards_of)[block_of(target)]
    other_side = (block_of(target) + shards_of // 2) % shards_of
    return jnp.where((block_of(source) == one_side) | (block_of(source) == other_side), factor * drawn, drawn)


def levels(rng, shape, shards, least, top_value):
    level = 1.0
    for position, shards_of in shards:
        draws = jax.random.uniform(jax.random.fold_in(jax.random.fold_in(rng, 6), position), (shards_of,), jnp.float32, least / len(shards), top_value / len(shards))
        level = level * jnp.repeat(jnp.exp(draws), shape[position] // shards_of).reshape((-1,) + (1,) * (len(shape) - 1 - position))
    return level


def gaussian(rng, extent, width, reach, split=(), held_as=jnp.bfloat16):
    values = width * jax.random.normal(rng, extent, jnp.float32)
    if split:
        values = values * levels(rng, extent, split, -0.22, 0.18)
    return jnp.clip(values, -reach, reach).astype(held_as)


def noise_with(own_key, dims, width, reach, cuts, heavy, kind=jnp.bfloat16):
    values = width * jax.random.normal(own_key, dims, jnp.float32)
    if cuts:
        values = values * levels(own_key, dims, cuts, -0.22, 0.18)
    return jnp.clip(raised(values, jax.random.fold_in(own_key, 3), *heavy), -reach, reach).astype(kind)


def setup_inputs(seed: int = 0) -> dict:
    key_list = jax.random.split(jax.random.key(seed), 9)
    return {
        "layer_input": noise_with(key_list[0], (REPLICAS, BATCH, SEQ, D), 1.0, 6.0, ((0, 32), (2, 16)), (2, 3, 16, 2.0)),
        "grad_out": gaussian(key_list[1], (REPLICAS, BATCH, SEQ, D), 1.0, 6.0, ((0, 32), (2, 16))),
        "gate_weight": gaussian(key_list[2], (D, D), D ** -0.5, 0.21875, ((0, 16),)),
        "mix_in_right": gaussian(key_list[3], (BLOCK, BLOCK, BLOCK), BLOCK ** -0.5, 0.75, ((0, 16),)),
        "mix_in_left": gaussian(key_list[4], (BLOCK, BLOCK, BLOCK), BLOCK ** -0.5, 0.75, ((0, 16),)),
        "mix_out_left": gaussian(key_list[5], (BLOCK, BLOCK, BLOCK), BLOCK ** -0.5, 0.75, ((0, 16),)),
        "mix_out_right": gaussian(key_list[6], (BLOCK, BLOCK, BLOCK), BLOCK ** -0.5, 0.75, ((0, 16),)),
        "kernel": gaussian(key_list[7], (SEQ, D), 1.0, 5.0, ((0, 16),)),
    }


def mix_product(form, left, right):
    return jnp.einsum(form, left.astype(jnp.float32), right.astype(jnp.float32))

def one_replica(inputs, gate_weight, right_in, left_in, left_out, right_out, kernel):
    layer_input, grad_out = inputs
    count_batch = layer_input.shape[0]
    acts = layer_input.reshape(count_batch, BLOCK, BLOCK, D)
    kern = kernel.reshape(BLOCK, BLOCK, D).astype(jnp.float32)
    first_mixed = mix_product('aic,bacd->baid', right_in, acts).astype(jnp.bfloat16)
    second_mixed = mix_product('ija,baid->bijd', left_in, first_mixed)
    weighted = (second_mixed * kern).astype(jnp.bfloat16)
    third_mixed = mix_product('ikj,bijd->bikd', left_out, weighted).astype(jnp.bfloat16)
    mixed = mix_product('kmi,bikd->bkmd', right_out, third_mixed).reshape(count_batch * SEQ, D)
    flat_input = layer_input.reshape(count_batch * SEQ, D)
    upstream = grad_out.reshape(count_batch * SEQ, D).astype(jnp.float32)
    preact = jnp.dot(flat_input, gate_weight, preferred_element_type=jnp.float32)
    sigma = jax.nn.sigmoid(preact)
    swish = preact * sigma
    slope = sigma * (1.0 + preact * (1.0 - sigma))
    mix_grad = (upstream * swish).astype(jnp.bfloat16).reshape(count_batch, BLOCK, BLOCK, D)
    gate_grad = (upstream * mixed * slope).astype(jnp.bfloat16)
    weight_sum = jnp.dot(flat_input.T, gate_grad, preferred_element_type=jnp.float32)
    gate_part = jnp.dot(gate_grad, gate_weight.T, preferred_element_type=jnp.float32)
    back_third = mix_product('kmi,bkmd->bkid', right_out, mix_grad).astype(jnp.bfloat16)
    back_second = mix_product('ikj,bkid->bijd', left_out, back_third)
    kernel_sum = lax.optimization_barrier(jnp.sum(second_mixed * back_second, axis=0)).reshape(SEQ, D)
    back_weighted = (back_second * kern).astype(jnp.bfloat16)
    back_first = mix_product('ija,bijd->biad', left_in, back_weighted).astype(jnp.bfloat16)
    mix_part = mix_product('aic,biad->bacd', right_in, back_first).reshape(count_batch * SEQ, D)
    input_grad = (gate_part + mix_part).astype(jnp.bfloat16).reshape(count_batch, SEQ, D)
    return (input_grad, weight_sum, kernel_sum)

def reference(layer_input, grad_out, gate_weight, mix_in_right, mix_in_left, mix_out_left, mix_out_right, kernel):

    def run_one(inputs):
        return one_replica(inputs, gate_weight, mix_in_right, mix_in_left, mix_out_left, mix_out_right, kernel)
    input_grad, weight_sums, kernel_sums = lax.map(run_one, (layer_input, grad_out))
    weight_grad = lax.optimization_barrier(jnp.sum(weight_sums, axis=0)) * (1.0 / math.sqrt(REPLICAS * BATCH * SEQ))
    kernel_grad = (lax.optimization_barrier(jnp.sum(kernel_sums, axis=0)) * (1.0 / math.sqrt(REPLICAS * BATCH))).astype(jnp.bfloat16)
    return (input_grad, weight_grad, kernel_grad)
```

```python
import math

import jax
import jax.numpy as jnp
from jax import lax
from jax.experimental import pallas as pl
from jax.experimental.pallas import tpu as pltpu
from jax.sharding import PartitionSpec as P

MESH = pl.DeviceIdType.MESH
BF16 = jnp.bfloat16
F32 = jnp.float32

PEERS = 16
BATCH = 3
ROWS = 256
WIDTH = 768
HALF = WIDTH // 2
TILE = 256
SHARD = WIDTH // PEERS
CHUNK = 512

FIRST, THIRD, BACK_THIRD, BACK_FIRST = 0, 1, 2, 3
IN_RIGHT, IN_LEFT, OUT_LEFT, OUT_RIGHT = 0, 1, 2, 3


def product(left, right, contract=((1,), (0,))):
    return lax.dot_general(left, right, (contract, ((), ())), preferred_element_type=F32)


def rows_of(index, size):
    return pl.ds(pl.multiple_of(index * size, size), size)


def mixer(
    x_any,
    g_any,
    w_any,
    in_right,
    in_left,
    out_left,
    out_right,
    kern_any,
    grad_any,
    weight_out,
    kernel_out,
    x,
    g,
    w,
    kern,
    mats,
    sent,
    got,
    second,
    slope,
    gate,
    grad,
    ksum,
    term,
    term_out,
    term_in,
    term_sent,
    term_got,
    kern_out,
    kern_in,
    z_sent,
    z_got,
    z_all,
    local_sem,
    send_sem,
    recv_sem,
    one_send,
    one_recv,
):
    section = lax.axis_index("section")
    me = lax.axis_index("seq")
    core = lax.rem(section, 2)
    level = lax.div(section, 2)
    other = 1 - core
    sibling = (2 * level + other, me)

    def seq_peer(step):
        return lax.rem(me + step, PEERS)

    def z_peer(step):
        return lax.rem(level + step, PEERS)

    my_half = pl.ds(pl.multiple_of(core * HALF, HALF), HALF)
    other_half = pl.ds(pl.multiple_of(other * HALF, HALF), HALF)
    loads = [
        pltpu.make_async_copy(x_any, x, local_sem.at[0]),
        pltpu.make_async_copy(
            w_any.at[:, my_half], w.at[rows_of(me, SHARD), my_half], local_sem.at[1]
        ),
        pltpu.make_async_copy(g_any, g, local_sem.at[2]),
        pltpu.make_async_copy(kern_any, kern, local_sem.at[3]),
    ]
    for load in loads:
        load.start()

    barrier = pltpu.get_barrier_semaphore()

    @pl.loop(1, PEERS)
    def _(step):
        pl.semaphore_signal(barrier, inc=1, device_id=(section, seq_peer(step)), device_id_type=MESH)
        pl.semaphore_signal(
            barrier, inc=1, device_id=(2 * z_peer(step) + core, me), device_id_type=MESH
        )

    pl.semaphore_signal(barrier, inc=1, device_id=sibling, device_id_type=MESH)

    row = lax.broadcasted_iota(jnp.int32, (ROWS, ROWS), 0)
    col = lax.broadcasted_iota(jnp.int32, (ROWS, ROWS), 1)
    small_row = lax.broadcasted_iota(jnp.int32, (64, ROWS), 0)
    small_col = lax.broadcasted_iota(jnp.int32, (64, ROWS), 1)
    order = jnp.where(col == (row & 3) * 64 + (row >> 2), 1.0, 0.0).astype(BF16)
    repeat = jnp.where(small_row == (small_col & 63), 1.0, 0.0).astype(BF16)
    spread = jnp.where(small_row == (small_col >> 4) * 4 + (small_col & 3), 1.0, 0.0).astype(BF16)
    on_block = (row >> 6) == (col >> 6)
    on_spread = (row >> 6) == ((col >> 2) & 3)
    for slot, factor in ((IN_RIGHT, in_right), (OUT_LEFT, out_left)):
        blocks = jnp.where(on_block, product(factor[...], repeat), 0.0).astype(BF16)
        matrix = product(order, blocks)
        mats[slot] = matrix.astype(BF16)
        mats[slot + 4] = matrix.T.astype(BF16)
    for slot, factor in ((IN_LEFT, in_left), (OUT_RIGHT, out_right)):
        matrix = jnp.where(on_spread, product(factor[...], spread), 0.0)
        mats[slot] = matrix.astype(BF16)
        mats[slot + 4] = matrix.T.astype(BF16)

    pl.semaphore_wait(barrier, 2 * (PEERS - 1) + 1)

    def exchange(which, b):
        @pl.loop(1, PEERS)
        def _(step):
            to = seq_peer(step)
            pltpu.make_async_remote_copy(
                sent.at[which, pl.ds(pl.multiple_of(b * ROWS + to * 16, 16), 16)],
                got.at[which, pl.ds(pl.multiple_of(b * ROWS + me * 16, 16), 16)],
                send_sem.at[which, b],
                recv_sem.at[which, b],
                device_id=(section, to),
                device_id_type=MESH,
            ).start()

        mine = pl.ds(pl.multiple_of(b * ROWS + me * 16, 16), 16)
        got[which, mine] = sent[which, mine]

    def exchanged(which, b):
        span = pl.ds(pl.multiple_of(b * ROWS, ROWS), ROWS - 16)
        return pltpu.make_async_remote_copy(
            sent.at[which, span],
            got.at[which, span],
            send_sem.at[which, b],
            recv_sem.at[which, b],
            device_id=(section, seq_peer(1)),
            device_id_type=MESH,
        )

    def single(source, target, slot, to):
        return pltpu.make_async_remote_copy(
            source, target, one_send.at[slot], one_recv.at[slot], device_id=to, device_id_type=MESH
        )

    tiles = [slice(at, at + TILE) for at in range(0, WIDTH, TILE)]

    loads[1].wait()

    @pl.loop(1, PEERS)
    def _(step):
        piece = w.at[rows_of(me, SHARD), my_half]
        single(piece, piece, 0, (section, seq_peer(step))).start()

    loads[0].wait()

    @pl.loop(0, BATCH)
    def _(b):
        here = rows_of(b, ROWS)
        for tile in tiles:
            sent[FIRST, here, tile] = product(mats[IN_RIGHT], x[here, tile]).astype(BF16)
        exchange(FIRST, b)

    most = w.at[pl.ds(0, WIDTH - SHARD), my_half]
    gathered = single(most, most, 0, (section, seq_peer(1)))
    gathered.wait_recv()
    half = w.at[:, my_half]
    paired = single(half, half, 1, sibling)
    paired.start()
    paired.wait_recv()
    loads[2].wait()
    loads[3].wait()

    @pl.loop(0, BATCH)
    def _(b):
        here = rows_of(b, ROWS)
        for tile in tiles:
            preact = product(x[here, :], w[:, tile])
            sigma = jax.nn.sigmoid(preact)
            upstream = g[here, tile].astype(F32)
            slope[here, tile] = upstream * (sigma * (1.0 + preact * (1.0 - sigma)))
            mix_grad = (upstream * (preact * sigma)).astype(BF16)
            sent[BACK_THIRD, here, tile] = product(mats[OUT_RIGHT + 4], mix_grad).astype(BF16)

    @pl.loop(0, BATCH)
    def _(b):
        here = rows_of(b, ROWS)
        exchanged(FIRST, b).wait_recv()
        for tile in tiles:
            mixed_in = product(mats[IN_LEFT], got[FIRST, here, tile])
            second[here, tile] = mixed_in
            weighted = (mixed_in * kern[:, tile].astype(F32)).astype(BF16)
            sent[THIRD, here, tile] = product(mats[OUT_LEFT], weighted).astype(BF16)
        exchange(THIRD, b)

    @pl.loop(0, BATCH)
    def _(b):
        exchange(BACK_THIRD, b)

    @pl.loop(0, BATCH)
    def _(b):
        here = rows_of(b, ROWS)
        exchanged(THIRD, b).wait_recv()
        for tile in tiles:
            mixed = product(mats[OUT_RIGHT], got[THIRD, here, tile])
            gate[here, tile] = (mixed * slope[here, tile]).astype(BF16)
        for tile in tiles:
            slope[here, tile] = product(gate[here, :], w[tile, :], ((1,), (1,)))

    for tile in tiles:
        term_out[tile, :] = product(x[:, tile], gate[:, other_half], ((0,), (0,))).astype(BF16)
    swapped = single(term_out, term_in, 2, sibling)
    swapped.start()
    for tile in tiles:
        term[tile, :] = product(x[:, tile], gate[:, my_half], ((0,), (0,)))
    swapped.wait_recv()
    term_sent[...] = (term[...] + term_in[...].astype(F32)).astype(BF16)

    @pl.loop(1, PEERS)
    def _(step):
        to = seq_peer(step)
        single(
            term_sent.at[rows_of(to, SHARD)], term_got.at[rows_of(me, SHARD)], 3, (section, to)
        ).start()

    term_got[rows_of(me, SHARD)] = term_sent[rows_of(me, SHARD)]

    ksum[...] = jnp.zeros_like(ksum)

    @pl.loop(0, BATCH)
    def _(b):
        here = rows_of(b, ROWS)
        exchanged(BACK_THIRD, b).wait_recv()
        for tile in tiles:
            back_second = product(mats[OUT_LEFT + 4], got[BACK_THIRD, here, tile])
            ksum[:, tile] += second[here, tile] * back_second
            back_weighted = (back_second * kern[:, tile].astype(F32)).astype(BF16)
            sent[BACK_FIRST, here, tile] = product(mats[IN_LEFT + 4], back_weighted).astype(BF16)
        exchange(BACK_FIRST, b)

    kern_out[...] = ksum[rows_of(other, ROWS // 2)].astype(BF16)
    kern_swap = single(kern_out, kern_in, 4, sibling)
    kern_swap.start()

    spans = pl.ds(0, WIDTH - SHARD)
    scattered = single(term_sent.at[spans], term_got.at[spans], 3, (section, seq_peer(1)))
    scattered.wait_recv()
    rows = term_got[0:SHARD].astype(F32)
    for source in range(1, PEERS):
        rows += term_got[source * SHARD : (source + 1) * SHARD].astype(F32)
    z_sent[:, :, HALF:] = jnp.zeros((PEERS, 16, CHUNK - HALF), BF16)
    for part in range(9):
        down, across = (part // 3) * 16, (part % 3) * 128
        z_sent[part, :, HALF:] = rows[down : down + 16, across : across + 128].astype(BF16)

    kern_swap.wait_recv()
    half_sum = ksum[rows_of(core, ROWS // 2)] + kern_in[...].astype(F32)
    for part in range(PEERS):
        down, across = (part // 2) * 16, (part % 2) * HALF
        z_sent[part, :, :HALF] = half_sum[down : down + 16, across : across + HALF].astype(BF16)

    @pl.loop(1, PEERS)
    def _(step):
        to = z_peer(step)
        single(z_sent.at[to], z_got.at[level], 5, (2 * to + core, me)).start()

    z_got[level] = z_sent[level]
    z_span = pl.ds(0, PEERS - 1)
    next_level = (2 * z_peer(1) + core, me)
    reduced = single(z_sent.at[z_span], z_got.at[z_span], 5, next_level)
    reduced.wait_recv()
    chunk = z_got[0].astype(F32)
    for source in range(1, PEERS):
        chunk += z_got[source].astype(F32)
    replicas = 2 * PEERS
    z_all[core, level, :, :HALF] = (chunk[:, :HALF] * (1.0 / math.sqrt(replicas * BATCH))).astype(BF16)
    z_all[core, level, :, HALF:] = (
        chunk[:, HALF:] * (1.0 / math.sqrt(replicas * BATCH * PEERS * ROWS))
    ).astype(BF16)

    @pl.loop(1, PEERS)
    def _(step):
        piece = z_all.at[core, level]
        single(piece, piece, 6, (2 * z_peer(step) + core, me)).start()

    stores = []
    for b in range(BATCH):
        here = slice(b * ROWS, (b + 1) * ROWS)
        exchanged(BACK_FIRST, b).wait_recv()
        for tile in tiles:
            mix_part = product(mats[IN_RIGHT + 4], got[BACK_FIRST, here, tile])
            grad[here, tile] = (slope[here, tile] + mix_part).astype(BF16)
        store = pltpu.make_async_copy(grad.at[here], grad_any.at[here], local_sem.at[4 + b])
        store.start()
        stores.append(store)

    z_rest = z_all.at[core, z_span]
    collected = single(z_rest, z_rest, 6, next_level)
    collected.wait_recv()
    z_half = z_all.at[core]
    z_swap = single(z_half, z_half, 7, sibling)
    z_swap.start()
    z_swap.wait_recv()
    for side in range(2):
        for part in range(PEERS):
            down, across = side * (ROWS // 2) + (part // 2) * 16, (part % 2) * HALF
            kernel_out[down : down + 16, across : across + HALF] = z_all[side, part, :, :HALF]
        for part in range(9):
            down, across = (part // 3) * 16, side * HALF + (part % 3) * 128
            weight_out[down : down + 16, across : across + 128] = z_all[side, part, :, HALF:].astype(F32)

    for store in stores:
        store.wait()
    for done in (gathered, paired, swapped, scattered, kern_swap, reduced, collected, z_swap):
        done.wait_send()
    for which in range(4):

        @pl.loop(0, BATCH)
        def _(b):
            exchanged(which, b).wait_send()


def local(
    layer_input,
    grad_out,
    gate_weight,
    mix_in_right,
    mix_in_left,
    mix_out_left,
    mix_out_right,
    kernel,
):
    tokens = BATCH * ROWS
    anywhere = pl.BlockSpec(memory_space=pl.ANY)
    inside = pl.BlockSpec(memory_space=pltpu.VMEM)
    input_grad, weight_grad, kernel_grad = pl.pallas_call(
        mixer,
        out_shape=(
            jax.ShapeDtypeStruct((tokens, WIDTH), BF16),
            jax.ShapeDtypeStruct((SHARD, WIDTH), F32),
            jax.ShapeDtypeStruct((ROWS, WIDTH), BF16),
        ),
        in_specs=[anywhere] * 3 + [inside] * 4 + [anywhere],
        out_specs=(anywhere, inside, inside),
        scratch_shapes=[
            pltpu.VMEM((tokens, WIDTH), BF16),
            pltpu.VMEM((tokens, WIDTH), BF16),
            pltpu.VMEM((WIDTH, WIDTH), BF16),
            pltpu.VMEM((ROWS, WIDTH), BF16),
            pltpu.VMEM((8, ROWS, ROWS), BF16),
            pltpu.VMEM((4, tokens, WIDTH), BF16),
            pltpu.VMEM((4, tokens, WIDTH), BF16),
            pltpu.VMEM((tokens, WIDTH), F32),
            pltpu.VMEM((tokens, WIDTH), F32),
            pltpu.VMEM((tokens, WIDTH), BF16),
            pltpu.VMEM((tokens, WIDTH), BF16),
            pltpu.VMEM((ROWS, WIDTH), F32),
            pltpu.VMEM((WIDTH, HALF), F32),
            pltpu.VMEM((WIDTH, HALF), BF16),
            pltpu.VMEM((WIDTH, HALF), BF16),
            pltpu.VMEM((WIDTH, HALF), BF16),
            pltpu.VMEM((WIDTH, HALF), BF16),
            pltpu.VMEM((ROWS // 2, WIDTH), BF16),
            pltpu.VMEM((ROWS // 2, WIDTH), BF16),
            pltpu.VMEM((PEERS, 16, CHUNK), BF16),
            pltpu.VMEM((PEERS, 16, CHUNK), BF16),
            pltpu.VMEM((2, PEERS, 16, CHUNK), BF16),
            pltpu.SemaphoreType.DMA((7,)),
            pltpu.SemaphoreType.DMA((4, BATCH)),
            pltpu.SemaphoreType.DMA((4, BATCH)),
            pltpu.SemaphoreType.DMA((8,)),
            pltpu.SemaphoreType.DMA((8,)),
        ],
        compiler_params=pltpu.CompilerParams(
            collective_id=0, has_side_effects=True, vmem_limit_bytes=52 << 20
        ),
    )(
        layer_input.reshape(tokens, WIDTH),
        grad_out.reshape(tokens, WIDTH),
        gate_weight,
        mix_in_right.reshape(ROWS, 64),
        mix_in_left.reshape(ROWS, 64),
        mix_out_left.reshape(ROWS, 64),
        mix_out_right.reshape(ROWS, 64),
        kernel,
    )
    return (input_grad.reshape(1, BATCH, ROWS, WIDTH), weight_grad, kernel_grad)


def solution(mesh):
    placed = (
        P("section", None, "seq", None),
        P("section", None, "seq", None),
        P("seq", None),
        P("seq", None, None),
        P("seq", None, None),
        P("seq", None, None),
        P("seq", None, None),
        P("seq", None),
    )
    return jax.shard_map(
        local,
        mesh=mesh,
        in_specs=placed,
        out_specs=(P("section", None, "seq", None), P("seq", None), P("seq", None)),
        check_vma=False,
    )
```

```python
import math

import jax
import jax.numpy as jnp
from jax import lax
from jax.experimental import pallas as pl
from jax.experimental.pallas import tpu as pltpu
from jax.sharding import PartitionSpec as P

MESH = pl.DeviceIdType.MESH
BF16 = jnp.bfloat16
F32 = jnp.float32

PEERS = 16
BATCH = 3
ROWS = 256
WIDTH = 768
HALF = WIDTH // 2
TILE = 256
SHARD = WIDTH // PEERS

FIRST, THIRD, BACK_THIRD, BACK_FIRST = 0, 1, 2, 3
IN_RIGHT, IN_LEFT, OUT_LEFT, OUT_RIGHT = 0, 1, 2, 3


def product(left, right, contract=((1,), (0,))):
    return lax.dot_general(left, right, (contract, ((), ())), preferred_element_type=F32)


def rows_of(index, size):
    return pl.ds(pl.multiple_of(index * size, size), size)


def mixer(
    x_any,
    g_any,
    w_any,
    in_right_any,
    in_left_any,
    out_left_any,
    out_right_any,
    kern_any,
    grad,
    weight_out,
    kernel_out,
    x,
    g,
    w,
    kern,
    factors,
    mats,
    sent,
    got,
    second,
    slope,
    gate,
    ksum,
    term,
    term_out,
    term_in,
    term_sent,
    term_got,
    kern_out,
    kern_in,
    kern_sent,
    kern_got,
    kern_all,
    part_sent,
    part_got,
    part_all,
    local_sem,
    send_sem,
    recv_sem,
    one_send,
    one_recv,
):
    section = lax.axis_index("section")
    me = lax.axis_index("seq")
    core = lax.rem(section, 2)
    level = lax.div(section, 2)
    other = 1 - core
    sibling = (2 * level + other, me)

    def seq_peer(step):
        return lax.rem(me + step, PEERS)

    def z_peer(step):
        return lax.rem(level + step, PEERS)

    my_half = pl.ds(pl.multiple_of(core * HALF, HALF), HALF)
    other_half = pl.ds(pl.multiple_of(other * HALF, HALF), HALF)
    barrier = pltpu.get_barrier_semaphore()

    @pl.loop(1, PEERS)
    def _(step):
        pl.semaphore_signal(barrier, inc=1, device_id=(section, seq_peer(step)), device_id_type=MESH)
        pl.semaphore_signal(
            barrier, inc=1, device_id=(2 * z_peer(step) + core, me), device_id_type=MESH
        )

    pl.semaphore_signal(barrier, inc=1, device_id=sibling, device_id_type=MESH)

    loads = [
        pltpu.make_async_copy(source, target, local_sem.at[slot])
        for slot, (source, target) in enumerate(
            (
                (in_right_any, factors.at[IN_RIGHT]),
                (w_any.at[:, my_half], w.at[rows_of(me, SHARD), my_half]),
                (x_any, x),
                (in_left_any, factors.at[IN_LEFT]),
                (out_left_any, factors.at[OUT_LEFT]),
                (out_right_any, factors.at[OUT_RIGHT]),
                (g_any, g),
                (kern_any, kern),
            )
        )
    ]
    for load in loads:
        load.start()
    part_sent[...] = jnp.zeros_like(part_sent)
    row = lax.broadcasted_iota(jnp.int32, (ROWS, ROWS), 0)
    col = lax.broadcasted_iota(jnp.int32, (ROWS, ROWS), 1)
    small_row = lax.broadcasted_iota(jnp.int32, (64, ROWS), 0)
    small_col = lax.broadcasted_iota(jnp.int32, (64, ROWS), 1)
    order = jnp.where(col == (row & 3) * 64 + (row >> 2), 1.0, 0.0).astype(BF16)
    repeat = jnp.where(small_row == (small_col & 63), 1.0, 0.0).astype(BF16)
    spread = jnp.where(small_row == (small_col >> 4) * 4 + (small_col & 3), 1.0, 0.0).astype(BF16)
    on_block = (row >> 6) == (col >> 6)
    on_spread = (row >> 6) == ((col >> 2) & 3)

    def ordered(slot):
        blocks = jnp.where(on_block, product(factors[slot], repeat), 0.0).astype(BF16)
        matrix = product(order, blocks)
        mats[slot] = matrix.astype(BF16)
        mats[slot + 4] = matrix.T.astype(BF16)

    def spaced(slot):
        matrix = jnp.where(on_spread, product(factors[slot], spread), 0.0)
        mats[slot] = matrix.astype(BF16)
        mats[slot + 4] = matrix.T.astype(BF16)

    loads[0].wait()
    ordered(IN_RIGHT)
    loads[1].wait()
    loads[2].wait()
    pl.semaphore_wait(barrier, 2 * (PEERS - 1) + 1)

    def exchange(which, b):
        @pl.loop(1, PEERS)
        def _(step):
            to = seq_peer(step)
            pltpu.make_async_remote_copy(
                sent.at[which, pl.ds(pl.multiple_of(b * ROWS + to * 16, 16), 16)],
                got.at[which, pl.ds(pl.multiple_of(b * ROWS + me * 16, 16), 16)],
                send_sem.at[which, b],
                recv_sem.at[which, b],
                device_id=(section, to),
                device_id_type=MESH,
            ).start()

        mine = pl.ds(pl.multiple_of(b * ROWS + me * 16, 16), 16)
        got[which, mine] = sent[which, mine]

    def exchanged(which, b):
        span = pl.ds(pl.multiple_of(b * ROWS, ROWS), ROWS - 16)
        return pltpu.make_async_remote_copy(
            sent.at[which, span],
            got.at[which, span],
            send_sem.at[which, b],
            recv_sem.at[which, b],
            device_id=(section, seq_peer(1)),
            device_id_type=MESH,
        )

    def single(source, target, slot, to):
        return pltpu.make_async_remote_copy(
            source, target, one_send.at[slot], one_recv.at[slot], device_id=to, device_id_type=MESH
        )

    tiles = [slice(at, at + TILE) for at in range(0, WIDTH, TILE)]
    @pl.loop(1, PEERS)
    def _(step):
        piece = w.at[rows_of(me, SHARD), my_half]
        single(piece, piece, 0, (section, seq_peer(step))).start()
    @pl.loop(0, BATCH)
    def _(b):
        here = rows_of(b, ROWS)
        for tile in tiles:
            sent[FIRST, here, tile] = product(mats[IN_RIGHT], x[here, tile]).astype(BF16)
        exchange(FIRST, b)
    for load in loads[3:]:
        load.wait()
    spaced(IN_LEFT)
    ordered(OUT_LEFT)
    spaced(OUT_RIGHT)
    most = w.at[pl.ds(0, WIDTH - SHARD), my_half]
    gathered = single(most, most, 0, (section, seq_peer(1)))
    gathered.wait_recv()
    half = w.at[:, my_half]
    paired = single(half, half, 1, sibling)
    paired.start()
    paired.wait_recv()
    @pl.loop(0, BATCH)
    def _(b):
        here = rows_of(b, ROWS)
        for tile in tiles:
            preact = product(x[here, :], w[:, tile])
            sigma = jax.nn.sigmoid(preact)
            upstream = g[here, tile].astype(F32)
            slope[here, tile] = upstream * (sigma * (1.0 + preact * (1.0 - sigma)))
            mix_grad = (upstream * (preact * sigma)).astype(BF16)
            sent[BACK_THIRD, here, tile] = product(mats[OUT_RIGHT + 4], mix_grad).astype(BF16)
        exchange(BACK_THIRD, b)
    @pl.loop(0, BATCH)
    def _(b):
        here = rows_of(b, ROWS)
        exchanged(FIRST, b).wait_recv()
        for tile in tiles:
            mixed_in = product(mats[IN_LEFT], got[FIRST, here, tile])
            second[here, tile] = mixed_in
            weighted = (mixed_in * kern[:, tile].astype(F32)).astype(BF16)
            sent[THIRD, here, tile] = product(mats[OUT_LEFT], weighted).astype(BF16)
        exchange(THIRD, b)
    ksum[...] = jnp.zeros_like(ksum)

    def back(b):
        here = rows_of(b, ROWS)
        exchanged(BACK_THIRD, b).wait_recv()
        for tile in tiles:
            back_second = product(mats[OUT_LEFT + 4], got[BACK_THIRD, here, tile])
            ksum[:, tile] += second[here, tile] * back_second
            back_weighted = (back_second * kern[:, tile].astype(F32)).astype(BF16)
            sent[BACK_FIRST, here, tile] = product(mats[IN_LEFT + 4], back_weighted).astype(BF16)

    @pl.loop(0, BATCH - 1)
    def _(b):
        back(b)
        exchange(BACK_FIRST, b)

    back(BATCH - 1)
    kern_out[...] = ksum[rows_of(other, ROWS // 2)].astype(BF16)
    kern_swap = single(kern_out, kern_in, 4, sibling)
    kern_swap.start()
    kern_swap.wait_recv()
    half_sum = ksum[rows_of(core, ROWS // 2)] + kern_in[...].astype(F32)
    for part in range(PEERS):
        down, across = (part // 2) * 16, (part % 2) * HALF
        kern_sent[part] = half_sum[down : down + 16, across : across + HALF].astype(BF16)

    @pl.loop(1, PEERS)
    def _(step):
        to = z_peer(step)
        single(kern_sent.at[to], kern_got.at[level], 5, (2 * to + core, me)).start()

    kern_got[level] = kern_sent[level]
    @pl.loop(0, BATCH)
    def _(b):
        here = rows_of(b, ROWS)
        exchanged(THIRD, b).wait_recv()
        for tile in tiles:
            mixed = product(mats[OUT_RIGHT], got[THIRD, here, tile])
            gate[here, tile] = (mixed * slope[here, tile]).astype(BF16)
    for tile in tiles:
        term_out[tile, :] = product(x[:, tile], gate[:, other_half], ((0,), (0,))).astype(BF16)
    swapped = single(term_out, term_in, 2, sibling)
    swapped.start()
    for tile in tiles:
        term[tile, :] = product(x[:, tile], gate[:, my_half], ((0,), (0,)))
    swapped.wait_recv()
    term_sent[...] = (term[...] + term_in[...].astype(F32)).astype(BF16)

    @pl.loop(1, PEERS)
    def _(step):
        to = seq_peer(step)
        single(
            term_sent.at[rows_of(to, SHARD)], term_got.at[rows_of(me, SHARD)], 3, (section, to)
        ).start()

    term_got[rows_of(me, SHARD)] = term_sent[rows_of(me, SHARD)]
    exchange(BACK_FIRST, BATCH - 1)
    replicas = 2 * PEERS
    z_span = pl.ds(0, PEERS - 1)
    next_level = (2 * z_peer(1) + core, me)
    reduced = single(kern_sent.at[z_span], kern_got.at[z_span], 5, next_level)
    reduced.wait_recv()
    chunk = kern_got[0].astype(F32)
    for source in range(1, PEERS):
        chunk += kern_got[source].astype(F32)
    kern_all[core, level] = (chunk * (1.0 / math.sqrt(replicas * BATCH))).astype(BF16)

    @pl.loop(1, PEERS)
    def _(step):
        piece = kern_all.at[core, level]
        single(piece, piece, 6, (2 * z_peer(step) + core, me)).start()
    @pl.loop(0, BATCH)
    def _(b):
        here = rows_of(b, ROWS)
        for tile in tiles:
            slope[here, tile] = product(gate[here, :], w[tile, :], ((1,), (1,)))
    spans = pl.ds(0, WIDTH - SHARD)
    scattered = single(term_sent.at[spans], term_got.at[spans], 3, (section, seq_peer(1)))
    scattered.wait_recv()
    rows = term_got[0:SHARD].astype(F32)
    for source in range(1, PEERS):
        rows += term_got[source * SHARD : (source + 1) * SHARD].astype(F32)
    for part in range(9):
        down, across = (part // 3) * 16, (part % 3) * 128
        part_sent[part] = rows[down : down + 16, across : across + 128].astype(BF16)

    @pl.loop(1, PEERS)
    def _(step):
        to = z_peer(step)
        single(part_sent.at[to], part_got.at[level], 7, (2 * to + core, me)).start()

    part_got[level] = part_sent[level]

    def finish(b):
        here = slice(b * ROWS, (b + 1) * ROWS)
        exchanged(BACK_FIRST, b).wait_recv()
        for tile in tiles:
            mix_part = product(mats[IN_RIGHT + 4], got[BACK_FIRST, here, tile])
            grad[here, tile] = (slope[here, tile] + mix_part).astype(BF16)
    finish(0)
    part_reduced = single(part_sent.at[z_span], part_got.at[z_span], 7, next_level)
    part_reduced.wait_recv()
    total = part_got[0].astype(F32)
    for source in range(1, PEERS):
        total += part_got[source].astype(F32)
    part_all[core, level] = (total * (1.0 / math.sqrt(replicas * BATCH * PEERS * ROWS))).astype(BF16)

    @pl.loop(1, PEERS)
    def _(step):
        piece = part_all.at[core, level]
        single(piece, piece, 8, (2 * z_peer(step) + core, me)).start()
    finish(1)
    kern_rest = kern_all.at[core, z_span]
    collected = single(kern_rest, kern_rest, 6, next_level)
    collected.wait_recv()
    kern_half = kern_all.at[core]
    kern_pair = single(kern_half, kern_half, 9, sibling)
    kern_pair.start()
    part_rest = part_all.at[core, z_span]
    part_collected = single(part_rest, part_rest, 8, next_level)
    part_collected.wait_recv()
    part_half = part_all.at[core, pl.ds(0, 9)]
    part_pair = single(part_half, part_half, 10, sibling)
    part_pair.start()
    finish(2)
    kern_pair.wait_recv()
    part_pair.wait_recv()
    for side in range(2):
        for part in range(PEERS):
            down, across = side * (ROWS // 2) + (part // 2) * 16, (part % 2) * HALF
            kernel_out[down : down + 16, across : across + HALF] = kern_all[side, part]
        for part in range(9):
            down, across = (part // 3) * 16, side * HALF + (part % 3) * 128
            weight_out[down : down + 16, across : across + 128] = part_all[side, part].astype(F32)
    for done in (
        gathered,
        paired,
        swapped,
        scattered,
        kern_swap,
        reduced,
        collected,
        part_reduced,
        part_collected,
        kern_pair,
        part_pair,
    ):
        done.wait_send()
    for which in range(4):

        @pl.loop(0, BATCH)
        def _(b):
            exchanged(which, b).wait_send()


def local(
    layer_input,
    grad_out,
    gate_weight,
    mix_in_right,
    mix_in_left,
    mix_out_left,
    mix_out_right,
    kernel,
):
    tokens = BATCH * ROWS
    outside = pl.BlockSpec(memory_space=pltpu.MemorySpace.HBM)
    inside = pl.BlockSpec(memory_space=pltpu.VMEM)
    input_grad, weight_grad, kernel_grad = pl.pallas_call(
        mixer,
        out_shape=(
            jax.ShapeDtypeStruct((tokens, WIDTH), BF16),
            jax.ShapeDtypeStruct((SHARD, WIDTH), F32),
            jax.ShapeDtypeStruct((ROWS, WIDTH), BF16),
        ),
        in_specs=[outside] * 8,
        out_specs=(inside, inside, inside),
        scratch_shapes=[
            pltpu.VMEM((tokens, WIDTH), BF16),
            pltpu.VMEM((tokens, WIDTH), BF16),
            pltpu.VMEM((WIDTH, WIDTH), BF16),
            pltpu.VMEM((ROWS, WIDTH), BF16),
            pltpu.VMEM((4, ROWS, 64), BF16),
            pltpu.VMEM((8, ROWS, ROWS), BF16),
            pltpu.VMEM((4, tokens, WIDTH), BF16),
            pltpu.VMEM((4, tokens, WIDTH), BF16),
            pltpu.VMEM((tokens, WIDTH), F32),
            pltpu.VMEM((tokens, WIDTH), F32),
            pltpu.VMEM((tokens, WIDTH), BF16),
            pltpu.VMEM((ROWS, WIDTH), F32),
            pltpu.VMEM((WIDTH, HALF), F32),
            pltpu.VMEM((WIDTH, HALF), BF16),
            pltpu.VMEM((WIDTH, HALF), BF16),
            pltpu.VMEM((WIDTH, HALF), BF16),
            pltpu.VMEM((WIDTH, HALF), BF16),
            pltpu.VMEM((ROWS // 2, WIDTH), BF16),
            pltpu.VMEM((ROWS // 2, WIDTH), BF16),
            pltpu.VMEM((PEERS, 16, HALF), BF16),
            pltpu.VMEM((PEERS, 16, HALF), BF16),
            pltpu.VMEM((2, PEERS, 16, HALF), BF16),
            pltpu.VMEM((PEERS, 16, 128), BF16),
            pltpu.VMEM((PEERS, 16, 128), BF16),
            pltpu.VMEM((2, PEERS, 16, 128), BF16),
            pltpu.SemaphoreType.DMA((8,)),
            pltpu.SemaphoreType.DMA((4, BATCH)),
            pltpu.SemaphoreType.DMA((4, BATCH)),
            pltpu.SemaphoreType.DMA((11,)),
            pltpu.SemaphoreType.DMA((11,)),
        ],
        compiler_params=pltpu.CompilerParams(
            collective_id=0, has_side_effects=True, vmem_limit_bytes=40 << 20
        ),
    )(
        *(
            pltpu.with_memory_space_constraint(value, pltpu.MemorySpace.HBM)
            for value in (
                layer_input.reshape(tokens, WIDTH),
                grad_out.reshape(tokens, WIDTH),
                gate_weight,
                mix_in_right.reshape(ROWS, 64),
                mix_in_left.reshape(ROWS, 64),
                mix_out_left.reshape(ROWS, 64),
                mix_out_right.reshape(ROWS, 64),
                kernel,
            )
        )
    )
    return (input_grad.reshape(1, BATCH, ROWS, WIDTH), weight_grad, kernel_grad)


def solution(mesh):
    placed = (
        P("section", None, "seq", None),
        P("section", None, "seq", None),
        P("seq", None),
        P("seq", None, None),
        P("seq", None, None),
        P("seq", None, None),
        P("seq", None, None),
        P("seq", None),
    )
    return jax.shard_map(
        local,
        mesh=mesh,
        in_specs=placed,
        out_specs=(P("section", None, "seq", None), P("seq", None), P("seq", None)),
        check_vma=False,
    )
```

```python
import math

import jax
import jax.numpy as jnp
from jax import lax
from jax.experimental import pallas as pl
from jax.experimental.pallas import tpu as pltpu
from jax.sharding import PartitionSpec as P

MESH = pl.DeviceIdType.MESH
BF16 = jnp.bfloat16
F32 = jnp.float32

PEERS = 16
BATCH = 3
ROWS = 256
WIDTH = 768
HALF = WIDTH // 2
TILE = 256
TILES = WIDTH // TILE
NEAR = 4
BLOCKS = 9
SHARD = WIDTH // PEERS

FIRST, THIRD, BACK_THIRD, BACK_FIRST = 0, 1, 2, 3
IN_RIGHT, IN_LEFT, OUT_LEFT, OUT_RIGHT = 0, 1, 2, 3


def product(left, right, contract=((1,), (0,))):
    return lax.dot_general(left, right, (contract, ((), ())), preferred_element_type=F32)


def rows_of(index, step, size=None):
    return pl.ds(pl.multiple_of(index * step, step), size or step)


def mixer(
    x_any,
    g_any,
    w_any,
    in_right_any,
    in_left_any,
    out_left_any,
    out_right_any,
    kern_any,
    grad,
    weight_out,
    kernel_out,
    x,
    flipped,
    g,
    w,
    kern,
    factors,
    mats,
    sent,
    got,
    second,
    slope,
    gate,
    ksum,
    kern_out,
    kern_in,
    kern_sent,
    kern_got,
    kern_all,
    term,
    term_out,
    term_in,
    term_sent,
    term_got,
    part_sent,
    part_got,
    part_all,
    local_sem,
    send_sem,
    recv_sem,
    one_send,
    one_recv,
    block_send,
    block_recv,
):
    section = lax.axis_index("section")
    me = lax.axis_index("seq")
    core = lax.rem(section, 2)
    level = lax.div(section, 2)
    other = 1 - core
    sibling = (2 * level + other, me)
    parity = lax.rem(level, 2)
    pair = (2 * (level + 1 - 2 * parity) + core, me)

    def seq_peer(step):
        shift = lax.rem(7 * step, PEERS)
        down = lax.rem(lax.div(me, NEAR) + lax.div(shift, NEAR), NEAR)
        return down * NEAR + lax.rem(me + shift, NEAR)

    def z_peer(step):
        return lax.rem(level + step, PEERS)

    group, place = lax.div(level, NEAR), lax.rem(level, NEAR)

    def near_peer(step):
        return group * NEAR + lax.rem(place + step, NEAR)

    def tile_of(index):
        return rows_of(index, TILE)

    def half_tile(index, side):
        return pl.ds(pl.multiple_of(index * TILE + side * 128, 128), 128)

    full = half_tile(2 * parity, core)
    middle = half_tile(1, core)

    def middle_rows(index):
        return pl.ds(pl.multiple_of(index * SHARD + parity * 16, 16), 32)
    barrier = pltpu.get_barrier_semaphore()

    @pl.loop(1, PEERS)
    def _(step):
        pl.semaphore_signal(barrier, inc=1, device_id=(section, seq_peer(step)), device_id_type=MESH)
        pl.semaphore_signal(
            barrier, inc=1, device_id=(2 * z_peer(step) + core, me), device_id_type=MESH
        )

    @pl.loop(0, NEAR)
    def _(step):
        pl.semaphore_signal(
            barrier, inc=1, device_id=(2 * near_peer(step) + other, me), device_id_type=MESH
        )

    loads = [
        pltpu.make_async_copy(source, target, local_sem.at[slot])
        for slot, (source, target) in enumerate(
            (
                (in_right_any, factors.at[IN_RIGHT]),
                (w_any.at[:, full], w.at[rows_of(me, SHARD), full]),
                (w_any.at[rows_of(parity, 16, 32), middle], w.at[middle_rows(me), middle]),
                (x_any, x),
                (in_left_any, factors.at[IN_LEFT]),
                (out_left_any, factors.at[OUT_LEFT]),
                (out_right_any, factors.at[OUT_RIGHT]),
                (g_any, g),
                (kern_any, kern),
            )
        )
    ]
    for load in loads:
        load.start()
    row = lax.broadcasted_iota(jnp.int32, (ROWS, ROWS), 0)
    col = lax.broadcasted_iota(jnp.int32, (ROWS, ROWS), 1)
    small_row = lax.broadcasted_iota(jnp.int32, (64, ROWS), 0)
    small_col = lax.broadcasted_iota(jnp.int32, (64, ROWS), 1)
    order = jnp.where(col == (row & 3) * 64 + (row >> 2), 1.0, 0.0).astype(BF16)
    repeat = jnp.where(small_row == (small_col & 63), 1.0, 0.0).astype(BF16)
    spread = jnp.where(small_row == (small_col >> 4) * 4 + (small_col & 3), 1.0, 0.0).astype(BF16)
    on_block = (row >> 6) == (col >> 6)
    on_spread = (row >> 6) == ((col >> 2) & 3)

    def ordered(slot):
        blocks = jnp.where(on_block, product(factors[slot], repeat), 0.0).astype(BF16)
        matrix = product(order, blocks)
        mats[slot] = matrix.astype(BF16)
        mats[slot + 4] = matrix.T.astype(BF16)

    def spaced(slot):
        matrix = jnp.where(on_spread, product(factors[slot], spread), 0.0)
        mats[slot] = matrix.astype(BF16)
        mats[slot + 4] = matrix.T.astype(BF16)

    loads[0].wait()
    ordered(IN_RIGHT)
    loads[1].wait()
    loads[2].wait()
    loads[3].wait()
    pl.semaphore_wait(barrier, 2 * (PEERS - 1) + NEAR)

    def exchange(which, tile):
        @pl.loop(1, PEERS)
        def _(step):
            to = seq_peer(step)
            pltpu.make_async_remote_copy(
                sent.at[which, tile, to],
                got.at[which, tile, me],
                send_sem.at[which, tile],
                recv_sem.at[which, tile],
                device_id=(section, to),
                device_id_type=MESH,
            ).start()

        got[which, tile, me] = sent[which, tile, me]

    def exchanged(which, tile):
        span = pl.ds(0, PEERS - 1)
        return pltpu.make_async_remote_copy(
            sent.at[which, tile, span],
            got.at[which, tile, span],
            send_sem.at[which, tile],
            recv_sem.at[which, tile],
            device_id=(section, seq_peer(1)),
            device_id_type=MESH,
        )

    def put(which, tile, b, value):
        sent[which, tile, :, b] = value.astype(BF16).reshape(PEERS, 16, TILE)

    def take(which, tile, b):
        return got[which, tile, :, b].reshape(ROWS, TILE)

    def single(source, target, slot, to):
        return pltpu.make_async_remote_copy(
            source, target, one_send.at[slot], one_recv.at[slot], device_id=to, device_id_type=MESH
        )

    spans = [slice(at, at + ROWS) for at in range(0, BATCH * ROWS, ROWS)]
    next_seq = (section, seq_peer(1))
    next_level = (2 * z_peer(1) + core, me)
    z_span = pl.ds(0, PEERS - 1)
    @pl.loop(1, PEERS)
    def _(step):
        piece = w.at[rows_of(me, SHARD), full]
        single(piece, piece, 0, (section, seq_peer(step))).start()
        piece = w.at[middle_rows(me), middle]
        single(piece, piece, 2, (section, seq_peer(step))).start()
    @pl.loop(0, TILES)
    def _(tile):
        for b, here in enumerate(spans):
            put(FIRST, tile, b, product(mats[IN_RIGHT], x[here, tile_of(tile)]))
        exchange(FIRST, tile)
    for load in loads[4:]:
        load.wait()
    spaced(IN_LEFT)
    ordered(OUT_LEFT)
    spaced(OUT_RIGHT)
    for here in spans:
        for tile in spans:
            flipped[tile, here] = x[here, tile].T
    most = w.at[pl.ds(0, WIDTH - SHARD), full]
    gathered = single(most, most, 0, next_seq)
    gathered.wait_recv()
    most = w.at[pl.ds(0, 32 * (PEERS - 1)), middle]
    gathered_middle = single(most, most, 2, next_seq)
    gathered_middle.wait_recv()
    piece = w.at[:, full]
    crossed = single(piece, piece, 3, pair)
    crossed.start()

    @pl.loop(0, PEERS)
    def _(source):
        piece = w.at[pl.ds(pl.multiple_of(source * SHARD + parity * 32, 16), 16), middle]
        single(piece, piece, 4, pair).start()
    crossed.wait_recv()
    some = w.at[pl.ds(0, 16 * PEERS), middle]
    crossed_middle = single(some, some, 4, pair)
    crossed_middle.wait_recv()
    for tile in range(TILES):
        piece = w.at[:, half_tile(tile, core)]
        single(piece, piece, 1, sibling).start()
    half = w.at[:, pl.ds(0, HALF)]
    paired = single(half, half, 1, sibling)
    paired.wait_recv()
    @pl.loop(0, TILES)
    def _(tile):
        for b, here in enumerate(spans):
            preact = product(x[here, :], w[:, tile_of(tile)])
            sigma = jax.nn.sigmoid(preact)
            upstream = g[here, tile_of(tile)].astype(F32)
            slope[here, tile_of(tile)] = upstream * (sigma * (1.0 + preact * (1.0 - sigma)))
            mix_grad = (upstream * (preact * sigma)).astype(BF16)
            put(BACK_THIRD, tile, b, product(mats[OUT_RIGHT + 4], mix_grad))
        exchange(BACK_THIRD, tile)
    @pl.loop(0, TILES)
    def _(tile):
        exchanged(FIRST, tile).wait_recv()
        kernel = kern[:, tile_of(tile)].astype(F32)
        for b, here in enumerate(spans):
            mixed_in = product(mats[IN_LEFT], take(FIRST, tile, b))
            second[here, tile_of(tile)] = mixed_in
            weighted = (mixed_in * kernel).astype(BF16)
            put(THIRD, tile, b, product(mats[OUT_LEFT], weighted))
        exchange(THIRD, tile)

    def back(tile):
        exchanged(BACK_THIRD, tile).wait_recv()
        kernel = kern[:, tile_of(tile)].astype(F32)
        for b, here in enumerate(spans):
            back_second = product(mats[OUT_LEFT + 4], take(BACK_THIRD, tile, b))
            change = second[here, tile_of(tile)] * back_second
            if b == 0:
                ksum[tile] = change
            else:
                ksum[tile] += change
            back_weighted = (back_second * kernel).astype(BF16)
            put(BACK_FIRST, tile, b, product(mats[IN_LEFT + 4], back_weighted))
        kern_out[tile] = ksum[tile, rows_of(other, ROWS // 2)].astype(BF16)
        swap = single(kern_out.at[tile], kern_in.at[tile], 5 + tile, sibling)
        swap.start()
        return swap

    def kern_scatter(tile):
        kern_swaps[tile].wait_recv()
        half_sum = ksum[tile, rows_of(core, ROWS // 2)] + kern_in[tile].astype(F32)
        for part in range(PEERS):
            down, across = (part // 2) * 16, (part % 2) * 128
            kern_sent[tile, part] = half_sum[down : down + 16, across : across + 128].astype(BF16)

        @pl.loop(1, PEERS)
        def _(step):
            to = z_peer(step)
            single(
                kern_sent.at[tile, to], kern_got.at[tile, level], 8 + tile, (2 * to + core, me)
            ).start()

        kern_got[tile, level] = kern_sent[tile, level]

    replicas = 2 * PEERS

    def kern_gather(tile):
        reduced[tile].wait_recv()
        chunk = kern_got[tile, 0].astype(F32)
        for source in range(1, PEERS):
            chunk += kern_got[tile, source].astype(F32)
        kern_all[core, level, tile] = (chunk * (1.0 / math.sqrt(replicas * BATCH))).astype(BF16)

        @pl.loop(1, PEERS)
        def _(step):
            piece = kern_all.at[core, level, tile]
            single(piece, piece, 11, (2 * z_peer(step) + core, me)).start()

    reduced = [
        single(kern_sent.at[tile, z_span], kern_got.at[tile, z_span], 8 + tile, next_level)
        for tile in range(TILES)
    ]
    kern_swaps = [back(0)]
    kern_swaps.append(back(1))
    kern_scatter(0)
    kern_swaps.append(back(2))
    kern_scatter(1)
    kern_scatter(2)

    def mix(tile):
        exchanged(THIRD, tile).wait_recv()
        for b, here in enumerate(spans):
            mixed = product(mats[OUT_RIGHT], take(THIRD, tile, b))
            gate[here, tile_of(tile)] = (mixed * slope[here, tile_of(tile)]).astype(BF16)
        for across in spans:
            term_out[tile, across] = product(
                flipped[across, :], gate[:, half_tile(tile, other)]
            ).astype(BF16)
        swap = single(term_out.at[tile], term_in.at[tile], 12 + tile, sibling)
        swap.start()
        for across in spans:
            term[tile, across] = product(flipped[across, :], gate[:, half_tile(tile, core)])
        return swap

    def term_scatter(tile):
        term_swaps[tile].wait_recv()
        term_sent[tile] = (term[tile] + term_in[tile].astype(F32)).astype(BF16)

        @pl.loop(1, PEERS)
        def _(step):
            to = seq_peer(step)
            single(
                term_sent.at[tile, rows_of(to, SHARD)],
                term_got.at[tile, rows_of(me, SHARD)],
                15 + tile,
                (section, to),
            ).start()

        term_got[tile, rows_of(me, SHARD)] = term_sent[tile, rows_of(me, SHARD)]
    term_swaps = [mix(0)]
    kern_gather(0)
    term_scatter(0)
    term_swaps.append(mix(1))
    kern_gather(1)
    term_scatter(1)
    term_swaps.append(mix(2))
    term_scatter(2)
    kern_gather(2)
    for here in spans:
        for tile in spans:
            slope[here, tile] = product(gate[here, :], w[tile, :], ((1,), (1,)))

    exchange(BACK_FIRST, 0)

    scattered = [
        single(
            term_sent.at[tile, pl.ds(0, WIDTH - SHARD)],
            term_got.at[tile, pl.ds(0, WIDTH - SHARD)],
            15 + tile,
            next_seq,
        )
        for tile in range(TILES)
    ]

    def part_scatter(tile):
        scattered[tile].wait_recv()
        rows = term_got[tile, 0:SHARD].astype(F32)
        for source in range(1, PEERS):
            rows += term_got[tile, source * SHARD : (source + 1) * SHARD].astype(F32)
        for down in range(3):
            part_sent[3 * down + tile] = rows[down * 16 : down * 16 + 16].astype(BF16)

        for block in range(tile, BLOCKS, 3):

            @pl.loop(0, PEERS // NEAR)
            def _(step):
                to = lax.rem(group + step, PEERS // NEAR) * NEAR + block % NEAR

                @pl.when(to != level)
                def _():
                    pltpu.make_async_remote_copy(
                        part_sent.at[block],
                        part_got.at[block // NEAR, level],
                        block_send.at[block],
                        block_recv.at[block // NEAR],
                        device_id=(2 * to + core, me),
                        device_id_type=MESH,
                    ).start()

            @pl.when(place == block % NEAR)
            def _():
                part_got[block // NEAR, level] = part_sent[block]

    def finish(tile):
        exchanged(BACK_FIRST, tile).wait_recv()
        for b, here in enumerate(spans):
            mix_part = product(mats[IN_RIGHT + 4], take(BACK_FIRST, tile, b))
            grad[here, tile_of(tile)] = (slope[here, tile_of(tile)] + mix_part).astype(BF16)
    part_scatter(0)
    part_scatter(1)
    part_scatter(2)
    exchange(BACK_FIRST, 1)
    finish(0)
    exchange(BACK_FIRST, 2)
    def part_gather(slot):
        block = slot * NEAR + place
        pltpu.make_async_remote_copy(
            part_got.at[slot, z_span],
            part_got.at[slot, z_span],
            block_send.at[0],
            block_recv.at[slot],
            device_id=next_level,
            device_id_type=MESH,
        ).wait_recv()
        total = part_got[slot, 0].astype(F32)
        for source in range(1, PEERS):
            total += part_got[slot, source].astype(F32)
        part_all[core, block] = (
            total * (1.0 / math.sqrt(replicas * BATCH * PEERS * ROWS))
        ).astype(BF16)
        piece = part_all.at[core, block]

        @pl.loop(1, NEAR)
        def _(step):
            single(piece, piece, 18, (2 * near_peer(step) + core, me)).start()

        @pl.loop(0, NEAR)
        def _(step):
            single(piece, piece, 18, (2 * near_peer(step) + other, me)).start()

    part_gather(0)
    part_gather(1)

    @pl.when(place == 0)
    def _():
        part_gather(2)
    kern_rest = kern_all.at[core, z_span]
    collected = single(kern_rest, kern_rest, 11, next_level)
    collected.wait_recv()
    kern_half = kern_all.at[core]
    kern_pair = single(kern_half, kern_half, 20, sibling)
    kern_pair.start()
    finish(1)
    kern_pair.wait_recv()
    for side in range(2):
        for part in range(PEERS):
            for tile in range(TILES):
                down, across = side * (ROWS // 2) + (part // 2) * 16, tile * TILE + (part % 2) * 128
                kernel_out[down : down + 16, across : across + 128] = kern_all[side, part, tile]
    finish(2)
    @pl.when(place == 0)
    def _():
        most = kern_all.at[0, pl.ds(0, 5)]
        single(most, most, 18, next_level).wait_recv()

    @pl.when(place != 0)
    def _():
        most = part_got.at[0]
        single(most, most, 18, next_level).wait_recv()
    for side in range(2):
        for part in range(BLOCKS):
            down, across = (part // 3) * 16, (part % 3) * TILE + side * 128
            weight_out[down : down + 16, across : across + 128] = part_all[side, part].astype(F32)
    for done in (
        gathered,
        gathered_middle,
        crossed,
        crossed_middle,
        paired,
        *kern_swaps,
        *reduced,
        *term_swaps,
        *scattered,
        collected,
        kern_pair,
    ):
        done.wait_send()

    for block in range(BLOCKS):

        def block_sent(pieces):
            pltpu.make_async_remote_copy(
                part_sent.at[pl.ds(0, pieces)],
                part_sent.at[pl.ds(0, pieces)],
                block_send.at[block],
                block_recv.at[0],
                device_id=next_level,
                device_id_type=MESH,
            ).wait_send()

        @pl.when(place == block % NEAR)
        def _():
            block_sent(3)

        @pl.when(place != block % NEAR)
        def _():
            block_sent(4)

    @pl.when(place == 0)
    def _():
        most = kern_all.at[0, pl.ds(0, 7)]
        single(most, most, 18, next_level).wait_send()

    @pl.when(place != 0)
    def _():
        most = part_got.at[0, pl.ds(0, 14)]
        single(most, most, 18, next_level).wait_send()

    for which in range(4):

        @pl.loop(0, TILES)
        def _(tile):
            exchanged(which, tile).wait_send()


def local(
    layer_input,
    grad_out,
    gate_weight,
    mix_in_right,
    mix_in_left,
    mix_out_left,
    mix_out_right,
    kernel,
):
    tokens = BATCH * ROWS
    outside = pl.BlockSpec(memory_space=pltpu.MemorySpace.HBM)
    inside = pl.BlockSpec(memory_space=pltpu.VMEM)
    input_grad, weight_grad, kernel_grad = pl.pallas_call(
        mixer,
        out_shape=(
            jax.ShapeDtypeStruct((tokens, WIDTH), BF16),
            jax.ShapeDtypeStruct((SHARD, WIDTH), F32),
            jax.ShapeDtypeStruct((ROWS, WIDTH), BF16),
        ),
        in_specs=[outside] * 8,
        out_specs=(inside, inside, inside),
        scratch_shapes=[
            pltpu.VMEM((tokens, WIDTH), BF16),
            pltpu.VMEM((WIDTH, tokens), BF16),
            pltpu.VMEM((tokens, WIDTH), BF16),
            pltpu.VMEM((WIDTH, WIDTH), BF16),
            pltpu.VMEM((ROWS, WIDTH), BF16),
            pltpu.VMEM((4, ROWS, 64), BF16),
            pltpu.VMEM((8, ROWS, ROWS), BF16),
            pltpu.VMEM((4, TILES, PEERS, BATCH, 16, TILE), BF16),
            pltpu.VMEM((4, TILES, PEERS, BATCH, 16, TILE), BF16),
            pltpu.VMEM((tokens, WIDTH), F32),
            pltpu.VMEM((tokens, WIDTH), F32),
            pltpu.VMEM((tokens, WIDTH), BF16),
            pltpu.VMEM((TILES, ROWS, TILE), F32),
            pltpu.VMEM((TILES, ROWS // 2, TILE), BF16),
            pltpu.VMEM((TILES, ROWS // 2, TILE), BF16),
            pltpu.VMEM((TILES, PEERS, 16, 128), BF16),
            pltpu.VMEM((TILES, PEERS, 16, 128), BF16),
            pltpu.VMEM((2, PEERS, TILES, 16, 128), BF16),
            pltpu.VMEM((TILES, WIDTH, 128), F32),
            pltpu.VMEM((TILES, WIDTH, 128), BF16),
            pltpu.VMEM((TILES, WIDTH, 128), BF16),
            pltpu.VMEM((TILES, WIDTH, 128), BF16),
            pltpu.VMEM((TILES, WIDTH, 128), BF16),
            pltpu.VMEM((BLOCKS, 16, 128), BF16),
            pltpu.VMEM((3, PEERS, 16, 128), BF16),
            pltpu.VMEM((2, BLOCKS, 16, 128), BF16),
            pltpu.SemaphoreType.DMA((9,)),
            pltpu.SemaphoreType.DMA((4, TILES)),
            pltpu.SemaphoreType.DMA((4, TILES)),
            pltpu.SemaphoreType.DMA((21,)),
            pltpu.SemaphoreType.DMA((21,)),
            pltpu.SemaphoreType.DMA((BLOCKS,)),
            pltpu.SemaphoreType.DMA((3,)),
        ],
        compiler_params=pltpu.CompilerParams(
            collective_id=0, has_side_effects=True, vmem_limit_bytes=40 << 20
        ),
    )(
        *(
            pltpu.with_memory_space_constraint(value, pltpu.MemorySpace.HBM)
            for value in (
                layer_input.reshape(tokens, WIDTH),
                grad_out.reshape(tokens, WIDTH),
                gate_weight,
                mix_in_right.reshape(ROWS, 64),
                mix_in_left.reshape(ROWS, 64),
                mix_out_left.reshape(ROWS, 64),
                mix_out_right.reshape(ROWS, 64),
                kernel,
            )
        )
    )
    return (input_grad.reshape(1, BATCH, ROWS, WIDTH), weight_grad, kernel_grad)


def solution(mesh):
    placed = (
        P("section", None, "seq", None),
        P("section", None, "seq", None),
        P("seq", None),
        P("seq", None, None),
        P("seq", None, None),
        P("seq", None, None),
        P("seq", None, None),
        P("seq", None),
    )
    return jax.shard_map(
        local,
        mesh=mesh,
        in_specs=placed,
        out_specs=(P("section", None, "seq", None), P("seq", None), P("seq", None)),
        check_vma=False,
    )
```

```python
import math

import jax
import jax.numpy as jnp
from jax import lax
from jax.experimental import pallas as pl
from jax.experimental.pallas import tpu as pltpu
from jax.sharding import PartitionSpec as P

MESH = pl.DeviceIdType.MESH
BF16 = jnp.bfloat16
F32 = jnp.float32

PEERS = 16
BATCH = 3
ROWS = 256
WIDTH = 768
HALF = WIDTH // 2
TILE = 256
TILES = WIDTH // TILE
NEAR = 4
BLOCKS = 9
SHARD = WIDTH // PEERS

FIRST, THIRD, BACK_THIRD, BACK_FIRST = 0, 1, 2, 3
IN_RIGHT, IN_LEFT, OUT_LEFT, OUT_RIGHT = 0, 1, 2, 3


def product(left, right, contract=((1,), (0,))):
    return lax.dot_general(left, right, (contract, ((), ())), preferred_element_type=F32)


def rows_of(index, step, size=None):
    return pl.ds(pl.multiple_of(index * step, step), size or step)


def mixer(
    x_any,
    g_any,
    w_any,
    in_right_any,
    in_left_any,
    out_left_any,
    out_right_any,
    kern_any,
    grad,
    weight_out,
    kernel_out,
    x,
    flipped,
    g,
    w,
    kern,
    factors,
    mats,
    sent,
    got,
    second,
    slope,
    gate,
    ksum,
    kern_out,
    kern_in,
    kern_sent,
    kern_got,
    kern_all,
    term,
    term_out,
    term_in,
    term_sent,
    term_got,
    part_sent,
    part_got,
    part_all,
    local_sem,
    send_sem,
    recv_sem,
    one_send,
    one_recv,
    block_send,
    block_recv,
    ready,
):
    section = lax.axis_index("section")
    me = lax.axis_index("seq")
    core = lax.rem(section, 2)
    level = lax.div(section, 2)
    other = 1 - core
    sibling = (2 * level + other, me)
    parity = lax.rem(level, 2)
    pair = (2 * (level + 1 - 2 * parity) + core, me)

    def seq_peer(step):
        shift = lax.rem(7 * (step + core * (PEERS - 2 * step)), PEERS)
        down = lax.rem(lax.div(me, NEAR) + lax.div(shift, NEAR), NEAR)
        return down * NEAR + lax.rem(me + shift, NEAR)

    def z_peer(step):
        away = lax.div(step, 2) * (1 - 2 * lax.rem(step, 2)) * (1 - 2 * core)
        return lax.rem(level + PEERS + PEERS // 2 + away, PEERS)

    group, place = lax.div(level, NEAR), lax.rem(level, NEAR)

    def near_peer(step):
        return group * NEAR + lax.rem(place + step, NEAR)

    def tile_of(index):
        return rows_of(index, TILE)

    def half_tile(index, side):
        return pl.ds(pl.multiple_of(index * TILE + side * 128, 128), 128)

    full = half_tile(2 * parity, core)
    middle = half_tile(1, core)

    def middle_rows(index):
        return pl.ds(pl.multiple_of(index * SHARD + parity * 16, 16), 32)
    barrier = pltpu.get_barrier_semaphore()

    @pl.loop(1, PEERS)
    def _(step):
        pl.semaphore_signal(barrier, inc=1, device_id=(section, seq_peer(step)), device_id_type=MESH)

    pl.semaphore_signal(barrier, inc=1, device_id=sibling, device_id_type=MESH)

    def level_to(away):
        return (2 * lax.rem(level + away, PEERS) + core, me)

    @pl.when(level < PEERS - 1)
    def _():
        pl.semaphore_signal(barrier, inc=1, device_id=level_to(1), device_id_type=MESH)

    @pl.when(level > 0)
    def _():
        pl.semaphore_signal(barrier, inc=1, device_id=level_to(PEERS - 1), device_id_type=MESH)

    loads = [
        pltpu.make_async_copy(source, target, local_sem.at[slot])
        for slot, (source, target) in enumerate(
            (
                (in_right_any, factors.at[IN_RIGHT]),
                (w_any.at[:, full], w.at[rows_of(me, SHARD), full]),
                (w_any.at[rows_of(parity, 16, 32), middle], w.at[middle_rows(me), middle]),
                (x_any, x),
                (in_left_any, factors.at[IN_LEFT]),
                (out_left_any, factors.at[OUT_LEFT]),
                (out_right_any, factors.at[OUT_RIGHT]),
                (g_any, g),
                (kern_any, kern),
            )
        )
    ]
    for load in loads:
        load.start()
    row = lax.broadcasted_iota(jnp.int32, (ROWS, ROWS), 0)
    col = lax.broadcasted_iota(jnp.int32, (ROWS, ROWS), 1)
    small_row = lax.broadcasted_iota(jnp.int32, (64, ROWS), 0)
    small_col = lax.broadcasted_iota(jnp.int32, (64, ROWS), 1)
    order = jnp.where(col == (row & 3) * 64 + (row >> 2), 1.0, 0.0).astype(BF16)
    repeat = jnp.where(small_row == (small_col & 63), 1.0, 0.0).astype(BF16)
    spread = jnp.where(small_row == (small_col >> 4) * 4 + (small_col & 3), 1.0, 0.0).astype(BF16)
    on_block = (row >> 6) == (col >> 6)
    on_spread = (row >> 6) == ((col >> 2) & 3)

    def ordered(slot):
        blocks = jnp.where(on_block, product(factors[slot], repeat), 0.0).astype(BF16)
        matrix = product(order, blocks)
        mats[slot] = matrix.astype(BF16)
        mats[slot + 4] = matrix.T.astype(BF16)

    def spaced(slot):
        matrix = jnp.where(on_spread, product(factors[slot], spread), 0.0)
        mats[slot] = matrix.astype(BF16)
        mats[slot + 4] = matrix.T.astype(BF16)

    loads[0].wait()
    ordered(IN_RIGHT)
    loads[1].wait()
    loads[2].wait()
    loads[3].wait()
    ends = jnp.where(jnp.logical_or(level == 0, level == PEERS - 1), 1, 0)
    pl.semaphore_wait(barrier, PEERS - 1 + 3 - ends)

    def pass_on(turn):
        away = 2**turn

        @pl.when(level < PEERS - away)
        def _():
            pl.semaphore_signal(ready.at[turn, 0], inc=1, device_id=level_to(away), device_id_type=MESH)

        @pl.when(level >= away)
        def _():
            pl.semaphore_signal(
                ready.at[turn, 1], inc=1, device_id=level_to(PEERS - away), device_id_type=MESH
            )

    def passed(turn):
        away = 2**turn

        @pl.when(level >= away)
        def _():
            pl.semaphore_wait(ready.at[turn, 0], 1)

        @pl.when(level < PEERS - away)
        def _():
            pl.semaphore_wait(ready.at[turn, 1], 1)

    def exchange(which, tile):
        @pl.loop(1, PEERS)
        def _(step):
            to = seq_peer(step)
            pltpu.make_async_remote_copy(
                sent.at[which, tile, to],
                got.at[which, tile, me],
                send_sem.at[which, tile],
                recv_sem.at[which, tile],
                device_id=(section, to),
                device_id_type=MESH,
            ).start()

        got[which, tile, me] = sent[which, tile, me]

    def exchanged(which, tile):
        span = pl.ds(0, PEERS - 1)
        return pltpu.make_async_remote_copy(
            sent.at[which, tile, span],
            got.at[which, tile, span],
            send_sem.at[which, tile],
            recv_sem.at[which, tile],
            device_id=(section, seq_peer(1)),
            device_id_type=MESH,
        )

    def put(which, tile, b, value):
        sent[which, tile, :, b] = value.astype(BF16).reshape(PEERS, 16, TILE)

    def take(which, tile, b):
        return got[which, tile, :, b].reshape(ROWS, TILE)

    def single(source, target, slot, to):
        return pltpu.make_async_remote_copy(
            source, target, one_send.at[slot], one_recv.at[slot], device_id=to, device_id_type=MESH
        )

    spans = [slice(at, at + ROWS) for at in range(0, BATCH * ROWS, ROWS)]
    next_seq = (section, seq_peer(1))
    next_level = (2 * z_peer(1) + core, me)
    z_span = pl.ds(0, PEERS - 1)
    @pl.loop(1, PEERS)
    def _(step):
        piece = w.at[rows_of(me, SHARD), full]
        single(piece, piece, 0, (section, seq_peer(step))).start()
        piece = w.at[middle_rows(me), middle]
        single(piece, piece, 2, (section, seq_peer(step))).start()
    @pl.loop(0, TILES)
    def _(tile):
        for b, here in enumerate(spans):
            put(FIRST, tile, b, product(mats[IN_RIGHT], x[here, tile_of(tile)]))
        exchange(FIRST, tile)

    pass_on(0)
    for load in loads[4:]:
        load.wait()
    spaced(IN_LEFT)
    ordered(OUT_LEFT)
    spaced(OUT_RIGHT)
    for here in spans:
        for tile in spans:
            flipped[tile, here] = x[here, tile].T
    most = w.at[pl.ds(0, WIDTH - SHARD), full]
    gathered = single(most, most, 0, next_seq)
    gathered.wait_recv()
    most = w.at[pl.ds(0, 32 * (PEERS - 1)), middle]
    gathered_middle = single(most, most, 2, next_seq)
    gathered_middle.wait_recv()
    piece = w.at[:, full]
    crossed = single(piece, piece, 3, pair)
    crossed.start()

    @pl.loop(0, PEERS)
    def _(source):
        piece = w.at[pl.ds(pl.multiple_of(source * SHARD + parity * 32, 16), 16), middle]
        single(piece, piece, 4, pair).start()
    crossed.wait_recv()
    some = w.at[pl.ds(0, 16 * PEERS), middle]
    crossed_middle = single(some, some, 4, pair)
    crossed_middle.wait_recv()
    for tile in range(TILES):
        piece = w.at[:, half_tile(tile, core)]
        single(piece, piece, 1, sibling).start()
    half = w.at[:, pl.ds(0, HALF)]
    paired = single(half, half, 1, sibling)
    paired.wait_recv()
    @pl.loop(0, TILES)
    def _(tile):
        for b, here in enumerate(spans):
            preact = product(x[here, :], w[:, tile_of(tile)])
            sigma = jax.nn.sigmoid(preact)
            upstream = g[here, tile_of(tile)].astype(F32)
            slope[here, tile_of(tile)] = upstream * (sigma * (1.0 + preact * (1.0 - sigma)))
            mix_grad = (upstream * (preact * sigma)).astype(BF16)
            put(BACK_THIRD, tile, b, product(mats[OUT_RIGHT + 4], mix_grad))
        exchange(BACK_THIRD, tile)

    passed(0)
    pass_on(1)
    @pl.loop(0, TILES)
    def _(tile):
        exchanged(FIRST, tile).wait_recv()
        kernel = kern[:, tile_of(tile)].astype(F32)
        for b, here in enumerate(spans):
            mixed_in = product(mats[IN_LEFT], take(FIRST, tile, b))
            second[here, tile_of(tile)] = mixed_in
            weighted = (mixed_in * kernel).astype(BF16)
            put(THIRD, tile, b, product(mats[OUT_LEFT], weighted))
        exchange(THIRD, tile)

    def back(tile):
        exchanged(BACK_THIRD, tile).wait_recv()
        kernel = kern[:, tile_of(tile)].astype(F32)
        for b, here in enumerate(spans):
            back_second = product(mats[OUT_LEFT + 4], take(BACK_THIRD, tile, b))
            change = second[here, tile_of(tile)] * back_second
            if b == 0:
                ksum[tile] = change
            else:
                ksum[tile] += change
            back_weighted = (back_second * kernel).astype(BF16)
            put(BACK_FIRST, tile, b, product(mats[IN_LEFT + 4], back_weighted))
        kern_out[tile] = ksum[tile, rows_of(other, ROWS // 2)].astype(BF16)
        swap = single(kern_out.at[tile], kern_in.at[tile], 5 + tile, sibling)
        swap.start()
        return swap

    def kern_scatter(tile):
        kern_swaps[tile].wait_recv()
        half_sum = ksum[tile, rows_of(core, ROWS // 2)] + kern_in[tile].astype(F32)
        for part in range(PEERS):
            down, across = (part // 2) * 16, (part % 2) * 128
            kern_sent[tile, part] = half_sum[down : down + 16, across : across + 128].astype(BF16)

        @pl.loop(1, PEERS)
        def _(step):
            to = z_peer(step)
            single(
                kern_sent.at[tile, to], kern_got.at[tile, level], 8 + tile, (2 * to + core, me)
            ).start()

        kern_got[tile, level] = kern_sent[tile, level]

    replicas = 2 * PEERS

    def kern_gather(tile):
        reduced[tile].wait_recv()
        chunk = kern_got[tile, 0].astype(F32)
        for source in range(1, PEERS):
            chunk += kern_got[tile, source].astype(F32)
        kern_all[core, level, tile] = (chunk * (1.0 / math.sqrt(replicas * BATCH))).astype(BF16)

        @pl.loop(1, PEERS)
        def _(step):
            piece = kern_all.at[core, level, tile]
            single(piece, piece, 11, (2 * z_peer(step) + core, me)).start()

    reduced = [
        single(kern_sent.at[tile, z_span], kern_got.at[tile, z_span], 8 + tile, next_level)
        for tile in range(TILES)
    ]

    passed(1)
    pass_on(2)
    kern_swaps = [back(0)]
    passed(2)
    pass_on(3)
    kern_swaps.append(back(1))
    passed(3)
    kern_scatter(0)
    kern_swaps.append(back(2))
    kern_scatter(1)
    kern_scatter(2)

    def mix(tile):
        exchanged(THIRD, tile).wait_recv()
        for b, here in enumerate(spans):
            mixed = product(mats[OUT_RIGHT], take(THIRD, tile, b))
            gate[here, tile_of(tile)] = (mixed * slope[here, tile_of(tile)]).astype(BF16)
        for across in spans:
            term_out[tile, across] = product(
                flipped[across, :], gate[:, half_tile(tile, other)]
            ).astype(BF16)
        swap = single(term_out.at[tile], term_in.at[tile], 12 + tile, sibling)
        swap.start()
        for across in spans:
            term[tile, across] = product(flipped[across, :], gate[:, half_tile(tile, core)])
        return swap

    def term_scatter(tile):
        term_swaps[tile].wait_recv()
        term_sent[tile] = (term[tile] + term_in[tile].astype(F32)).astype(BF16)

        @pl.loop(1, PEERS)
        def _(step):
            to = seq_peer(step)
            single(
                term_sent.at[tile, rows_of(to, SHARD)],
                term_got.at[tile, rows_of(me, SHARD)],
                15 + tile,
                (section, to),
            ).start()

        term_got[tile, rows_of(me, SHARD)] = term_sent[tile, rows_of(me, SHARD)]
    term_swaps = [mix(0)]
    kern_gather(0)
    term_scatter(0)
    term_swaps.append(mix(1))
    kern_gather(1)
    term_scatter(1)
    term_swaps.append(mix(2))
    term_scatter(2)
    kern_gather(2)
    for here in spans:
        for tile in spans:
            slope[here, tile] = product(gate[here, :], w[tile, :], ((1,), (1,)))

    exchange(BACK_FIRST, 0)

    scattered = [
        single(
            term_sent.at[tile, pl.ds(0, WIDTH - SHARD)],
            term_got.at[tile, pl.ds(0, WIDTH - SHARD)],
            15 + tile,
            next_seq,
        )
        for tile in range(TILES)
    ]

    def part_scatter(tile):
        scattered[tile].wait_recv()
        rows = term_got[tile, 0:SHARD].astype(F32)
        for source in range(1, PEERS):
            rows += term_got[tile, source * SHARD : (source + 1) * SHARD].astype(F32)
        for down in range(3):
            part_sent[3 * down + tile] = rows[down * 16 : down * 16 + 16].astype(BF16)

        for block in range(tile, BLOCKS, 3):

            @pl.loop(0, PEERS // NEAR)
            def _(step):
                to = lax.rem(group + 2 + step, PEERS // NEAR) * NEAR + block % NEAR

                @pl.when(to != level)
                def _():
                    pltpu.make_async_remote_copy(
                        part_sent.at[block],
                        part_got.at[block // NEAR, level],
                        block_send.at[block],
                        block_recv.at[block // NEAR],
                        device_id=(2 * to + core, me),
                        device_id_type=MESH,
                    ).start()

            @pl.when(place == block % NEAR)
            def _():
                part_got[block // NEAR, level] = part_sent[block]

    def finish(tile):
        exchanged(BACK_FIRST, tile).wait_recv()
        for b, here in enumerate(spans):
            mix_part = product(mats[IN_RIGHT + 4], take(BACK_FIRST, tile, b))
            grad[here, tile_of(tile)] = (slope[here, tile_of(tile)] + mix_part).astype(BF16)
    part_scatter(0)
    part_scatter(1)
    part_scatter(2)
    exchange(BACK_FIRST, 1)
    finish(0)
    exchange(BACK_FIRST, 2)
    def part_gather(slot):
        block = slot * NEAR + place
        pltpu.make_async_remote_copy(
            part_got.at[slot, z_span],
            part_got.at[slot, z_span],
            block_send.at[0],
            block_recv.at[slot],
            device_id=next_level,
            device_id_type=MESH,
        ).wait_recv()
        total = part_got[slot, 0].astype(F32)
        for source in range(1, PEERS):
            total += part_got[slot, source].astype(F32)
        part_all[core, block] = (
            total * (1.0 / math.sqrt(replicas * BATCH * PEERS * ROWS))
        ).astype(BF16)
        piece = part_all.at[core, block]

        @pl.loop(1, NEAR)
        def _(step):
            single(piece, piece, 18, (2 * near_peer(step) + core, me)).start()

        @pl.loop(0, NEAR)
        def _(step):
            single(piece, piece, 18, (2 * near_peer(step) + other, me)).start()

    part_gather(0)
    part_gather(1)

    @pl.when(place == 0)
    def _():
        part_gather(2)
    kern_rest = kern_all.at[core, z_span]
    collected = single(kern_rest, kern_rest, 11, next_level)
    collected.wait_recv()
    kern_half = kern_all.at[core]
    kern_pair = single(kern_half, kern_half, 20, sibling)
    kern_pair.start()
    finish(1)
    kern_pair.wait_recv()
    for side in range(2):
        for part in range(PEERS):
            for tile in range(TILES):
                down, across = side * (ROWS // 2) + (part // 2) * 16, tile * TILE + (part % 2) * 128
                kernel_out[down : down + 16, across : across + 128] = kern_all[side, part, tile]
    finish(2)
    @pl.when(place == 0)
    def _():
        most = kern_all.at[0, pl.ds(0, 5)]
        single(most, most, 18, next_level).wait_recv()

    @pl.when(place != 0)
    def _():
        most = part_got.at[0]
        single(most, most, 18, next_level).wait_recv()
    for side in range(2):
        for part in range(BLOCKS):
            down, across = (part // 3) * 16, (part % 3) * TILE + side * 128
            weight_out[down : down + 16, across : across + 128] = part_all[side, part].astype(F32)
    for done in (
        gathered,
        gathered_middle,
        crossed,
        crossed_middle,
        paired,
        *kern_swaps,
        *reduced,
        *term_swaps,
        *scattered,
        collected,
        kern_pair,
    ):
        done.wait_send()

    for block in range(BLOCKS):

        def block_sent(pieces):
            pltpu.make_async_remote_copy(
                part_sent.at[pl.ds(0, pieces)],
                part_sent.at[pl.ds(0, pieces)],
                block_send.at[block],
                block_recv.at[0],
                device_id=next_level,
                device_id_type=MESH,
            ).wait_send()

        @pl.when(place == block % NEAR)
        def _():
            block_sent(3)

        @pl.when(place != block % NEAR)
        def _():
            block_sent(4)

    @pl.when(place == 0)
    def _():
        most = kern_all.at[0, pl.ds(0, 7)]
        single(most, most, 18, next_level).wait_send()

    @pl.when(place != 0)
    def _():
        most = part_got.at[0, pl.ds(0, 14)]
        single(most, most, 18, next_level).wait_send()

    for which in range(4):

        @pl.loop(0, TILES)
        def _(tile):
            exchanged(which, tile).wait_send()


def store(grad, weight, kernel, grad_any, weight_any, kernel_any, sems):
    copies = [
        pltpu.make_async_copy(source, target, sems.at[slot])
        for slot, (source, target) in enumerate(
            ((grad, grad_any), (kernel, kernel_any), (weight, weight_any))
        )
    ]
    for copy in copies:
        copy.start()
    for copy in copies:
        copy.wait()


def local(
    layer_input,
    grad_out,
    gate_weight,
    mix_in_right,
    mix_in_left,
    mix_out_left,
    mix_out_right,
    kernel,
):
    tokens = BATCH * ROWS
    outside = pl.BlockSpec(memory_space=pltpu.MemorySpace.HBM)
    inside = pl.BlockSpec(memory_space=pltpu.VMEM)
    input_grad, weight_grad, kernel_grad = pl.pallas_call(
        mixer,
        out_shape=(
            jax.ShapeDtypeStruct((tokens, WIDTH), BF16),
            jax.ShapeDtypeStruct((SHARD, WIDTH), F32),
            jax.ShapeDtypeStruct((ROWS, WIDTH), BF16),
        ),
        in_specs=[outside] * 8,
        out_specs=(inside, inside, inside),
        scratch_shapes=[
            pltpu.VMEM((tokens, WIDTH), BF16),
            pltpu.VMEM((WIDTH, tokens), BF16),
            pltpu.VMEM((tokens, WIDTH), BF16),
            pltpu.VMEM((WIDTH, WIDTH), BF16),
            pltpu.VMEM((ROWS, WIDTH), BF16),
            pltpu.VMEM((4, ROWS, 64), BF16),
            pltpu.VMEM((8, ROWS, ROWS), BF16),
            pltpu.VMEM((4, TILES, PEERS, BATCH, 16, TILE), BF16),
            pltpu.VMEM((4, TILES, PEERS, BATCH, 16, TILE), BF16),
            pltpu.VMEM((tokens, WIDTH), F32),
            pltpu.VMEM((tokens, WIDTH), F32),
            pltpu.VMEM((tokens, WIDTH), BF16),
            pltpu.VMEM((TILES, ROWS, TILE), F32),
            pltpu.VMEM((TILES, ROWS // 2, TILE), BF16),
            pltpu.VMEM((TILES, ROWS // 2, TILE), BF16),
            pltpu.VMEM((TILES, PEERS, 16, 128), BF16),
            pltpu.VMEM((TILES, PEERS, 16, 128), BF16),
            pltpu.VMEM((2, PEERS, TILES, 16, 128), BF16),
            pltpu.VMEM((TILES, WIDTH, 128), F32),
            pltpu.VMEM((TILES, WIDTH, 128), BF16),
            pltpu.VMEM((TILES, WIDTH, 128), BF16),
            pltpu.VMEM((TILES, WIDTH, 128), BF16),
            pltpu.VMEM((TILES, WIDTH, 128), BF16),
            pltpu.VMEM((BLOCKS, 16, 128), BF16),
            pltpu.VMEM((3, PEERS, 16, 128), BF16),
            pltpu.VMEM((2, BLOCKS, 16, 128), BF16),
            pltpu.SemaphoreType.DMA((9,)),
            pltpu.SemaphoreType.DMA((4, TILES)),
            pltpu.SemaphoreType.DMA((4, TILES)),
            pltpu.SemaphoreType.DMA((21,)),
            pltpu.SemaphoreType.DMA((21,)),
            pltpu.SemaphoreType.DMA((BLOCKS,)),
            pltpu.SemaphoreType.DMA((3,)),
            pltpu.SemaphoreType.REGULAR((4, 2)),
        ],
        compiler_params=pltpu.CompilerParams(
            collective_id=0, has_side_effects=True, vmem_limit_bytes=40 << 20
        ),
    )(
        *(
            pltpu.with_memory_space_constraint(value, pltpu.MemorySpace.HBM)
            for value in (
                layer_input.reshape(tokens, WIDTH),
                grad_out.reshape(tokens, WIDTH),
                gate_weight,
                mix_in_right.reshape(ROWS, 64),
                mix_in_left.reshape(ROWS, 64),
                mix_out_left.reshape(ROWS, 64),
                mix_out_right.reshape(ROWS, 64),
                kernel,
            )
        )
    )
    anywhere = pl.BlockSpec(memory_space=pl.ANY)
    input_grad, weight_grad, kernel_grad = pl.pallas_call(
        store,
        out_shape=tuple(
            jax.ShapeDtypeStruct(value.shape, value.dtype)
            for value in (input_grad, weight_grad, kernel_grad)
        ),
        in_specs=[anywhere] * 3,
        out_specs=(anywhere,) * 3,
        scratch_shapes=[pltpu.SemaphoreType.DMA((3,))],
        compiler_params=pltpu.CompilerParams(vmem_limit_bytes=1 << 20),
    )(input_grad, weight_grad, kernel_grad)
    return (input_grad.reshape(1, BATCH, ROWS, WIDTH), weight_grad, kernel_grad)


def solution(mesh):
    placed = (
        P("section", None, "seq", None),
        P("section", None, "seq", None),
        P("seq", None),
        P("seq", None, None),
        P("seq", None, None),
        P("seq", None, None),
        P("seq", None, None),
        P("seq", None),
    )
    return jax.shard_map(
        local,
        mesh=mesh,
        in_specs=placed,
        out_specs=(P("section", None, "seq", None), P("seq", None), P("seq", None)),
        check_vma=False,
    )
```

```python
import math

import jax
import jax.numpy as jnp
from jax import lax
from jax.experimental import pallas as pl
from jax.experimental.pallas import tpu as pltpu
from jax.sharding import PartitionSpec as P

MESH = pl.DeviceIdType.MESH
BF16 = jnp.bfloat16
F32 = jnp.float32

PEERS = 16
BATCH = 3
ROWS = 256
WIDTH = 768
HALF = WIDTH // 2
TILE = 256
TILES = WIDTH // TILE
NEAR = 4
BLOCKS = 9
SHARD = WIDTH // PEERS

FIRST, THIRD, BACK_THIRD, BACK_FIRST = 0, 1, 2, 3
IN_RIGHT, IN_LEFT, OUT_LEFT, OUT_RIGHT = 0, 1, 2, 3


def product(left, right, contract=((1,), (0,))):
    return lax.dot_general(left, right, (contract, ((), ())), preferred_element_type=F32)


def rows_of(index, step, size=None):
    return pl.ds(pl.multiple_of(index * step, step), size or step)


def mixer(
    x_any,
    g_any,
    w_any,
    in_right_any,
    in_left_any,
    out_left_any,
    out_right_any,
    kern_any,
    grad,
    weight_out,
    kernel_out,
    x,
    flipped,
    g,
    w,
    kern,
    factors,
    mats,
    sent,
    got,
    second,
    slope,
    gate,
    ksum,
    kern_out,
    kern_in,
    kern_sent,
    kern_got,
    kern_all,
    term,
    term_out,
    term_in,
    term_sent,
    term_got,
    part_sent,
    part_got,
    part_all,
    local_sem,
    send_sem,
    recv_sem,
    one_send,
    one_recv,
    block_send,
    block_recv,
    ready,
):
    section = lax.axis_index("section")
    me = lax.axis_index("seq")
    core = lax.rem(section, 2)
    level = lax.div(section, 2)
    other = 1 - core
    sibling = (2 * level + other, me)
    parity = lax.rem(level, 2)
    pair = (2 * (level + 1 - 2 * parity) + core, me)

    def seq_peer(step):
        shift = lax.rem(7 * (step + core * (PEERS - 2 * step)), PEERS)
        down = lax.rem(lax.div(me, NEAR) + lax.div(shift, NEAR), NEAR)
        return down * NEAR + lax.rem(me + shift, NEAR)

    def z_peer(step):
        away = lax.div(step, 2) * (1 - 2 * lax.rem(step, 2)) * (1 - 2 * core)
        return lax.rem(level + PEERS + PEERS // 2 + away, PEERS)

    group, place = lax.div(level, NEAR), lax.rem(level, NEAR)

    def near_peer(step):
        return group * NEAR + lax.rem(place + step, NEAR)

    def tile_of(index):
        return rows_of(index, TILE)

    def half_tile(index, side):
        return pl.ds(pl.multiple_of(index * TILE + side * 128, 128), 128)

    full = half_tile(2 * parity, core)
    middle = half_tile(1, core)

    def middle_rows(index):
        return pl.ds(pl.multiple_of(index * SHARD + parity * 16, 16), 32)
    barrier = pltpu.get_barrier_semaphore()

    @pl.loop(1, PEERS)
    def _(step):
        pl.semaphore_signal(barrier, inc=1, device_id=(section, seq_peer(step)), device_id_type=MESH)

    pl.semaphore_signal(barrier, inc=1, device_id=sibling, device_id_type=MESH)

    def level_to(away):
        return (2 * lax.rem(level + away, PEERS) + core, me)

    @pl.when(level < PEERS - 1)
    def _():
        pl.semaphore_signal(barrier, inc=1, device_id=level_to(1), device_id_type=MESH)

    @pl.when(level > 0)
    def _():
        pl.semaphore_signal(barrier, inc=1, device_id=level_to(PEERS - 1), device_id_type=MESH)

    loads = [
        pltpu.make_async_copy(source, target, local_sem.at[slot])
        for slot, (source, target) in enumerate(
            (
                (in_right_any, factors.at[IN_RIGHT]),
                (w_any.at[:, full], w.at[rows_of(me, SHARD), full]),
                (w_any.at[rows_of(parity, 16, 32), middle], w.at[middle_rows(me), middle]),
                (x_any, x),
                (in_left_any, factors.at[IN_LEFT]),
                (out_left_any, factors.at[OUT_LEFT]),
                (out_right_any, factors.at[OUT_RIGHT]),
                (g_any, g),
                (kern_any, kern),
            )
        )
    ]
    for load in loads:
        load.start()
    row = lax.broadcasted_iota(jnp.int32, (ROWS, ROWS), 0)
    col = lax.broadcasted_iota(jnp.int32, (ROWS, ROWS), 1)
    small_row = lax.broadcasted_iota(jnp.int32, (64, ROWS), 0)
    small_col = lax.broadcasted_iota(jnp.int32, (64, ROWS), 1)
    order = jnp.where(col == (row & 3) * 64 + (row >> 2), 1.0, 0.0).astype(BF16)
    repeat = jnp.where(small_row == (small_col & 63), 1.0, 0.0).astype(BF16)
    spread = jnp.where(small_row == (small_col >> 4) * 4 + (small_col & 3), 1.0, 0.0).astype(BF16)
    on_block = (row >> 6) == (col >> 6)
    on_spread = (row >> 6) == ((col >> 2) & 3)

    def ordered(slot):
        blocks = jnp.where(on_block, product(factors[slot], repeat), 0.0).astype(BF16)
        matrix = product(order, blocks)
        mats[slot] = matrix.astype(BF16)
        mats[slot + 4] = matrix.T.astype(BF16)

    def spaced(slot):
        matrix = jnp.where(on_spread, product(factors[slot], spread), 0.0)
        mats[slot] = matrix.astype(BF16)
        mats[slot + 4] = matrix.T.astype(BF16)

    loads[0].wait()
    ordered(IN_RIGHT)
    loads[1].wait()
    loads[2].wait()
    loads[3].wait()
    ends = jnp.where(jnp.logical_or(level == 0, level == PEERS - 1), 1, 0)
    pl.semaphore_wait(barrier, PEERS - 1 + 3 - ends)

    def pass_on(turn):
        away = 2**turn

        @pl.when(level < PEERS - away)
        def _():
            pl.semaphore_signal(ready.at[turn, 0], inc=1, device_id=level_to(away), device_id_type=MESH)

        @pl.when(level >= away)
        def _():
            pl.semaphore_signal(
                ready.at[turn, 1], inc=1, device_id=level_to(PEERS - away), device_id_type=MESH
            )

    def passed(turn):
        away = 2**turn

        @pl.when(level >= away)
        def _():
            pl.semaphore_wait(ready.at[turn, 0], 1)

        @pl.when(level < PEERS - away)
        def _():
            pl.semaphore_wait(ready.at[turn, 1], 1)

    def exchange(which, tile):
        @pl.loop(1, PEERS)
        def _(step):
            to = seq_peer(step)
            pltpu.make_async_remote_copy(
                sent.at[which, tile, to],
                got.at[which, tile, me],
                send_sem.at[which, tile],
                recv_sem.at[which, tile],
                device_id=(section, to),
                device_id_type=MESH,
            ).start()

        got[which, tile, me] = sent[which, tile, me]

    def exchanged(which, tile):
        span = pl.ds(0, PEERS - 1)
        return pltpu.make_async_remote_copy(
            sent.at[which, tile, span],
            got.at[which, tile, span],
            send_sem.at[which, tile],
            recv_sem.at[which, tile],
            device_id=(section, seq_peer(1)),
            device_id_type=MESH,
        )

    def put(which, tile, b, value):
        sent[which, tile, :, b] = value.astype(BF16).reshape(PEERS, 16, TILE)

    def take(which, tile, b):
        return got[which, tile, :, b].reshape(ROWS, TILE)

    def single(source, target, slot, to):
        return pltpu.make_async_remote_copy(
            source, target, one_send.at[slot], one_recv.at[slot], device_id=to, device_id_type=MESH
        )

    spans = [slice(at, at + ROWS) for at in range(0, BATCH * ROWS, ROWS)]
    next_seq = (section, seq_peer(1))
    next_level = (2 * z_peer(1) + core, me)
    z_span = pl.ds(0, PEERS - 1)
    @pl.loop(1, PEERS)
    def _(step):
        piece = w.at[rows_of(me, SHARD), full]
        single(piece, piece, 0, (section, seq_peer(step))).start()
        piece = w.at[middle_rows(me), middle]
        single(piece, piece, 2, (section, seq_peer(step))).start()
    @pl.loop(0, TILES)
    def _(tile):
        for b, here in enumerate(spans):
            put(FIRST, tile, b, product(mats[IN_RIGHT], x[here, tile_of(tile)]))
        exchange(FIRST, tile)

    pass_on(0)
    for load in loads[4:]:
        load.wait()
    spaced(IN_LEFT)
    ordered(OUT_LEFT)
    spaced(OUT_RIGHT)
    for here in spans:
        for tile in spans:
            flipped[tile, here] = x[here, tile].T
    most = w.at[pl.ds(0, WIDTH - SHARD), full]
    gathered = single(most, most, 0, next_seq)
    gathered.wait_recv()
    most = w.at[pl.ds(0, 32 * (PEERS - 1)), middle]
    gathered_middle = single(most, most, 2, next_seq)
    gathered_middle.wait_recv()
    piece = w.at[:, full]
    crossed = single(piece, piece, 3, pair)
    crossed.start()

    @pl.loop(0, PEERS)
    def _(source):
        piece = w.at[pl.ds(pl.multiple_of(source * SHARD + parity * 32, 16), 16), middle]
        single(piece, piece, 4, pair).start()
    crossed.wait_recv()
    some = w.at[pl.ds(0, 16 * PEERS), middle]
    crossed_middle = single(some, some, 4, pair)
    crossed_middle.wait_recv()
    for tile in range(TILES):
        piece = w.at[:, half_tile(tile, core)]
        single(piece, piece, 1, sibling).start()
    half = w.at[:, pl.ds(0, HALF)]
    paired = single(half, half, 1, sibling)
    paired.wait_recv()
    @pl.loop(0, TILES)
    def _(tile):
        for b, here in enumerate(spans):
            preact = product(x[here, :], w[:, tile_of(tile)])
            sigma = jax.nn.sigmoid(preact)
            upstream = g[here, tile_of(tile)].astype(F32)
            slope[here, tile_of(tile)] = upstream * (sigma * (1.0 + preact * (1.0 - sigma)))
            mix_grad = (upstream * (preact * sigma)).astype(BF16)
            put(BACK_THIRD, tile, b, product(mats[OUT_RIGHT + 4], mix_grad))
        exchange(BACK_THIRD, tile)

    passed(0)
    pass_on(1)
    @pl.loop(0, TILES)
    def _(tile):
        exchanged(FIRST, tile).wait_recv()
        kernel = kern[:, tile_of(tile)].astype(F32)
        for b, here in enumerate(spans):
            mixed_in = product(mats[IN_LEFT], take(FIRST, tile, b))
            second[here, tile_of(tile)] = mixed_in
            weighted = (mixed_in * kernel).astype(BF16)
            put(THIRD, tile, b, product(mats[OUT_LEFT], weighted))
        exchange(THIRD, tile)

    def back(tile):
        exchanged(BACK_THIRD, tile).wait_recv()
        kernel = kern[:, tile_of(tile)].astype(F32)
        for b, here in enumerate(spans):
            back_second = product(mats[OUT_LEFT + 4], take(BACK_THIRD, tile, b))
            change = second[here, tile_of(tile)] * back_second
            if b == 0:
                ksum[tile] = change
            else:
                ksum[tile] += change
            back_weighted = (back_second * kernel).astype(BF16)
            put(BACK_FIRST, tile, b, product(mats[IN_LEFT + 4], back_weighted))
        kern_out[tile] = ksum[tile, rows_of(other, ROWS // 2)].astype(BF16)
        swap = single(kern_out.at[tile], kern_in.at[tile], 5 + tile, sibling)
        swap.start()
        return swap

    def kern_scatter(tile):
        kern_swaps[tile].wait_recv()
        half_sum = ksum[tile, rows_of(core, ROWS // 2)] + kern_in[tile].astype(F32)
        for part in range(PEERS):
            down, across = (part // 2) * 16, (part % 2) * 128
            kern_sent[tile, part] = half_sum[down : down + 16, across : across + 128].astype(BF16)

        @pl.loop(1, PEERS)
        def _(step):
            to = z_peer(step)
            single(
                kern_sent.at[tile, to], kern_got.at[tile, level], 8 + tile, (2 * to + core, me)
            ).start()

        kern_got[tile, level] = kern_sent[tile, level]

    replicas = 2 * PEERS

    def kern_gather(tile):
        reduced[tile].wait_recv()
        chunk = kern_got[tile, 0].astype(F32)
        for source in range(1, PEERS):
            chunk += kern_got[tile, source].astype(F32)
        kern_all[core, level, tile] = (chunk * (1.0 / math.sqrt(replicas * BATCH))).astype(BF16)

        @pl.loop(1, PEERS)
        def _(step):
            piece = kern_all.at[core, level, tile]
            single(piece, piece, 11, (2 * z_peer(step) + core, me)).start()

    reduced = [
        single(kern_sent.at[tile, z_span], kern_got.at[tile, z_span], 8 + tile, next_level)
        for tile in range(TILES)
    ]

    passed(1)
    pass_on(2)
    kern_swaps = [back(0)]
    passed(2)
    pass_on(3)
    kern_swaps.append(back(1))
    passed(3)
    kern_scatter(0)
    kern_swaps.append(back(2))
    kern_scatter(1)
    kern_scatter(2)

    def mix(tile):
        exchanged(THIRD, tile).wait_recv()
        for b, here in enumerate(spans):
            mixed = product(mats[OUT_RIGHT], take(THIRD, tile, b))
            gate[here, tile_of(tile)] = (mixed * slope[here, tile_of(tile)]).astype(BF16)
        for across in spans:
            term_out[tile, across] = product(
                flipped[across, :], gate[:, half_tile(tile, other)]
            ).astype(BF16)
        swap = single(term_out.at[tile], term_in.at[tile], 12 + tile, sibling)
        swap.start()
        for across in spans:
            term[tile, across] = product(flipped[across, :], gate[:, half_tile(tile, core)])
        return swap

    def term_scatter(tile):
        term_swaps[tile].wait_recv()
        term_sent[tile] = (term[tile] + term_in[tile].astype(F32)).astype(BF16)

        @pl.loop(1, PEERS)
        def _(step):
            to = seq_peer(step)
            single(
                term_sent.at[tile, rows_of(to, SHARD)],
                term_got.at[tile, rows_of(me, SHARD)],
                15 + tile,
                (section, to),
            ).start()

        term_got[tile, rows_of(me, SHARD)] = term_sent[tile, rows_of(me, SHARD)]
    term_swaps = [mix(0)]
    kern_gather(0)
    term_scatter(0)
    term_swaps.append(mix(1))
    kern_gather(1)
    term_scatter(1)
    term_swaps.append(mix(2))
    term_scatter(2)
    kern_gather(2)
    for here in spans:
        for tile in spans:
            slope[here, tile] = product(gate[here, :], w[tile, :], ((1,), (1,)))

    scattered = [
        single(
            term_sent.at[tile, pl.ds(0, WIDTH - SHARD)],
            term_got.at[tile, pl.ds(0, WIDTH - SHARD)],
            15 + tile,
            next_seq,
        )
        for tile in range(TILES)
    ]

    def part_scatter(tile):
        scattered[tile].wait_recv()
        rows = term_got[tile, 0:SHARD].astype(F32)
        for source in range(1, PEERS):
            rows += term_got[tile, source * SHARD : (source + 1) * SHARD].astype(F32)
        for down in range(3):
            part_sent[3 * down + tile] = rows[down * 16 : down * 16 + 16].astype(BF16)

        for block in range(tile, BLOCKS, 3):

            @pl.loop(0, PEERS // NEAR)
            def _(step):
                to = lax.rem(group + 2 + step, PEERS // NEAR) * NEAR + block % NEAR

                @pl.when(to != level)
                def _():
                    pltpu.make_async_remote_copy(
                        part_sent.at[block],
                        part_got.at[block // NEAR, level],
                        block_send.at[block],
                        block_recv.at[block // NEAR],
                        device_id=(2 * to + core, me),
                        device_id_type=MESH,
                    ).start()

            @pl.when(place == block % NEAR)
            def _():
                part_got[block // NEAR, level] = part_sent[block]

    def finish(tile):
        exchanged(BACK_FIRST, tile).wait_recv()
        for b, here in enumerate(spans):
            mix_part = product(mats[IN_RIGHT + 4], take(BACK_FIRST, tile, b))
            grad[here, tile_of(tile)] = (slope[here, tile_of(tile)] + mix_part).astype(BF16)
    part_scatter(0)
    part_scatter(1)
    part_scatter(2)
    exchange(BACK_FIRST, 0)
    exchange(BACK_FIRST, 1)
    finish(0)
    exchange(BACK_FIRST, 2)
    def part_gather(slot):
        block = slot * NEAR + place
        pltpu.make_async_remote_copy(
            part_got.at[slot, z_span],
            part_got.at[slot, z_span],
            block_send.at[0],
            block_recv.at[slot],
            device_id=next_level,
            device_id_type=MESH,
        ).wait_recv()
        total = part_got[slot, 0].astype(F32)
        for source in range(1, PEERS):
            total += part_got[slot, source].astype(F32)
        part_all[core, block] = (
            total * (1.0 / math.sqrt(replicas * BATCH * PEERS * ROWS))
        ).astype(BF16)
        piece = part_all.at[core, block]

        @pl.loop(1, NEAR)
        def _(step):
            single(piece, piece, 18, (2 * near_peer(step) + core, me)).start()

        @pl.loop(0, NEAR)
        def _(step):
            single(piece, piece, 18, (2 * near_peer(step) + other, me)).start()

    part_gather(0)
    part_gather(1)

    @pl.when(place == 0)
    def _():
        part_gather(2)
    kern_rest = kern_all.at[core, z_span]
    collected = single(kern_rest, kern_rest, 11, next_level)
    collected.wait_recv()
    kern_half = kern_all.at[core]
    kern_pair = single(kern_half, kern_half, 20, sibling)
    kern_pair.start()
    finish(1)
    kern_pair.wait_recv()
    for side in range(2):
        for part in range(PEERS):
            for tile in range(TILES):
                down, across = side * (ROWS // 2) + (part // 2) * 16, tile * TILE + (part % 2) * 128
                kernel_out[down : down + 16, across : across + 128] = kern_all[side, part, tile]
    finish(2)
    @pl.when(place == 0)
    def _():
        most = kern_all.at[0, pl.ds(0, 5)]
        single(most, most, 18, next_level).wait_recv()

    @pl.when(place != 0)
    def _():
        most = part_got.at[0]
        single(most, most, 18, next_level).wait_recv()
    for side in range(2):
        for part in range(BLOCKS):
            down, across = (part // 3) * 16, (part % 3) * TILE + side * 128
            weight_out[down : down + 16, across : across + 128] = part_all[side, part].astype(F32)
    for done in (
        gathered,
        gathered_middle,
        crossed,
        crossed_middle,
        paired,
        *kern_swaps,
        *reduced,
        *term_swaps,
        *scattered,
        collected,
        kern_pair,
    ):
        done.wait_send()

    for block in range(BLOCKS):

        def block_sent(pieces):
            pltpu.make_async_remote_copy(
                part_sent.at[pl.ds(0, pieces)],
                part_sent.at[pl.ds(0, pieces)],
                block_send.at[block],
                block_recv.at[0],
                device_id=next_level,
                device_id_type=MESH,
            ).wait_send()

        @pl.when(place == block % NEAR)
        def _():
            block_sent(3)

        @pl.when(place != block % NEAR)
        def _():
            block_sent(4)

    @pl.when(place == 0)
    def _():
        most = kern_all.at[0, pl.ds(0, 7)]
        single(most, most, 18, next_level).wait_send()

    @pl.when(place != 0)
    def _():
        most = part_got.at[0, pl.ds(0, 14)]
        single(most, most, 18, next_level).wait_send()

    for which in range(4):

        @pl.loop(0, TILES)
        def _(tile):
            exchanged(which, tile).wait_send()


def store(grad, weight, kernel, grad_any, weight_any, kernel_any, sems):
    copies = [
        pltpu.make_async_copy(source, target, sems.at[slot])
        for slot, (source, target) in enumerate(
            ((grad, grad_any), (kernel, kernel_any), (weight, weight_any))
        )
    ]
    for copy in copies:
        copy.start()
    for copy in copies:
        copy.wait()


def local(
    layer_input,
    grad_out,
    gate_weight,
    mix_in_right,
    mix_in_left,
    mix_out_left,
    mix_out_right,
    kernel,
):
    tokens = BATCH * ROWS
    outside = pl.BlockSpec(memory_space=pltpu.MemorySpace.HBM)
    inside = pl.BlockSpec(memory_space=pltpu.VMEM)
    input_grad, weight_grad, kernel_grad = pl.pallas_call(
        mixer,
        out_shape=(
            jax.ShapeDtypeStruct((tokens, WIDTH), BF16),
            jax.ShapeDtypeStruct((SHARD, WIDTH), F32),
            jax.ShapeDtypeStruct((ROWS, WIDTH), BF16),
        ),
        in_specs=[outside] * 8,
        out_specs=(inside, inside, inside),
        scratch_shapes=[
            pltpu.VMEM((tokens, WIDTH), BF16),
            pltpu.VMEM((WIDTH, tokens), BF16),
            pltpu.VMEM((tokens, WIDTH), BF16),
            pltpu.VMEM((WIDTH, WIDTH), BF16),
            pltpu.VMEM((ROWS, WIDTH), BF16),
            pltpu.VMEM((4, ROWS, 64), BF16),
            pltpu.VMEM((8, ROWS, ROWS), BF16),
            pltpu.VMEM((4, TILES, PEERS, BATCH, 16, TILE), BF16),
            pltpu.VMEM((4, TILES, PEERS, BATCH, 16, TILE), BF16),
            pltpu.VMEM((tokens, WIDTH), F32),
            pltpu.VMEM((tokens, WIDTH), F32),
            pltpu.VMEM((tokens, WIDTH), BF16),
            pltpu.VMEM((TILES, ROWS, TILE), F32),
            pltpu.VMEM((TILES, ROWS // 2, TILE), BF16),
            pltpu.VMEM((TILES, ROWS // 2, TILE), BF16),
            pltpu.VMEM((TILES, PEERS, 16, 128), BF16),
            pltpu.VMEM((TILES, PEERS, 16, 128), BF16),
            pltpu.VMEM((2, PEERS, TILES, 16, 128), BF16),
            pltpu.VMEM((TILES, WIDTH, 128), F32),
            pltpu.VMEM((TILES, WIDTH, 128), BF16),
            pltpu.VMEM((TILES, WIDTH, 128), BF16),
            pltpu.VMEM((TILES, WIDTH, 128), BF16),
            pltpu.VMEM((TILES, WIDTH, 128), BF16),
            pltpu.VMEM((BLOCKS, 16, 128), BF16),
            pltpu.VMEM((3, PEERS, 16, 128), BF16),
            pltpu.VMEM((2, BLOCKS, 16, 128), BF16),
            pltpu.SemaphoreType.DMA((9,)),
            pltpu.SemaphoreType.DMA((4, TILES)),
            pltpu.SemaphoreType.DMA((4, TILES)),
            pltpu.SemaphoreType.DMA((21,)),
            pltpu.SemaphoreType.DMA((21,)),
            pltpu.SemaphoreType.DMA((BLOCKS,)),
            pltpu.SemaphoreType.DMA((3,)),
            pltpu.SemaphoreType.REGULAR((4, 2)),
        ],
        compiler_params=pltpu.CompilerParams(
            collective_id=0, has_side_effects=True, vmem_limit_bytes=40 << 20
        ),
    )(
        *(
            pltpu.with_memory_space_constraint(value, pltpu.MemorySpace.HBM)
            for value in (
                layer_input.reshape(tokens, WIDTH),
                grad_out.reshape(tokens, WIDTH),
                gate_weight,
                mix_in_right.reshape(ROWS, 64),
                mix_in_left.reshape(ROWS, 64),
                mix_out_left.reshape(ROWS, 64),
                mix_out_right.reshape(ROWS, 64),
                kernel,
            )
        )
    )
    anywhere = pl.BlockSpec(memory_space=pl.ANY)
    input_grad, weight_grad, kernel_grad = pl.pallas_call(
        store,
        out_shape=tuple(
            jax.ShapeDtypeStruct(value.shape, value.dtype)
            for value in (input_grad, weight_grad, kernel_grad)
        ),
        in_specs=[anywhere] * 3,
        out_specs=(anywhere,) * 3,
        scratch_shapes=[pltpu.SemaphoreType.DMA((3,))],
        compiler_params=pltpu.CompilerParams(vmem_limit_bytes=1 << 20),
    )(input_grad, weight_grad, kernel_grad)
    return (input_grad.reshape(1, BATCH, ROWS, WIDTH), weight_grad, kernel_grad)


def solution(mesh):
    placed = (
        P("section", None, "seq", None),
        P("section", None, "seq", None),
        P("seq", None),
        P("seq", None, None),
        P("seq", None, None),
        P("seq", None, None),
        P("seq", None, None),
        P("seq", None),
    )
    return jax.shard_map(
        local,
        mesh=mesh,
        in_specs=placed,
        out_specs=(P("section", None, "seq", None), P("seq", None), P("seq", None)),
        check_vma=False,
    )
```
